32 devices in a mesh: grp: 2 (over core), tp: 8 (over z, y), dp: 2 (over x).
Axes of the slice: x: 2, y: 2, z: 4, core: 2. Of those that a mesh axis runs over, the one named last changes fastest.
Arguments:
- base_inputs: bfloat16 [3, 128, 8192], P(None, 'dp', ('grp', 'tp')), may hold values from -6 to 6
- small_inputs: bfloat16 [2, 3, 128, 4096], P('grp', None, 'dp', 'tp'), may hold values from -6 to 6
- base_norm_gain: float32 [8192], replicated, may hold values from 0.1 to 1.9
- base_query: bfloat16 [8192, 8192], P(None, ('grp', 'tp')), may hold values from -0.0625 to 0.0625
- base_keys_values: bfloat16 [2, 8192, 1024], P(None, None, ('grp', 'tp')), may hold values from -0.0625 to 0.0625
- base_output: bfloat16 [8192, 8192], P(('grp', 'tp')), may hold values from -0.0625 to 0.0625
- base_cache: bfloat16 [2, 128, 1024, 128], P(None, 'dp', ('grp', 'tp')), may hold values from -600 to 600
- base_final_gain: float32 [8192], replicated, may hold values from 0.1 to 1.9
- base_unembed: bfloat16 [16384, 8192], P(('grp', 'tp')), may hold values from -20 to 20
- small_norm_gain: float32 [2, 4096], P('grp'), may hold values from 0.1 to 1.9
- small_projections: bfloat16 [2, 3, 4096, 4096], P('grp', None, None, 'tp'), may hold values from -0.09375 to 0.09375
- small_output: bfloat16 [2, 4096, 4096], P('grp', 'tp'), may hold values from -0.09375 to 0.09375
- small_cache: bfloat16 [2, 2, 128, 4096, 128], P('grp', None, 'dp', 'tp'), may hold values from -600 to 600
- small_final_gain: float32 [2, 4096], P('grp'), may hold values from 0.1 to 1.9
- small_unembed: bfloat16 [2, 2, 8192, 4096], P('grp', None, 'tp'), may hold values from -0.1875 to 0.1875
- lengths: int32 [128], P('dp'), may hold values from 1 to 128, as said below
- next_tokens: int32 [3, 128], P(None, 'dp'), may hold values from 0 to 16383
Outputs:
- log_probs: float32 [3, 128, 16384], P(None, 'dp', ('grp', 'tp'))
- chosen_total: float32 [128], P('dp')
The draws below stay inside these ranges and needn't reach their ends.
Inputs may be any that keep to these rules, and one draw needn't show every extreme that they name: `lengths`: some row holds 128 cached positions.
All inputs are finite; a program needn't handle non-finite values.
Results may differ from the reference program's by a relative error of at most 0.0035.
Values may be sent and summed in bfloat16 or wider, within the bound.
A program may use at most 256 MiB of HBM per device.

```python
import math
import jax
import jax.numpy as jnp
from jax import lax

DB = 8192
HB = 64
KVB = 8
HD = 128
DS = 4096
HS = 32
VOCAB = 16384
STEPS = 3
CACHE = 128
ROWS = 128
N_GRP = 2
N_TP = 8


def cache_draw(key, full_shape):
    key_entries = jax.random.fold_in(key, 0)
    entries = jnp.clip(jax.random.normal(key_entries, full_shape, jnp.float32), -6.0, 6.0)
    key_factor = jnp.ones((ROWS, 1, CACHE), jnp.float32)
    factor = jnp.stack([key_factor, jnp.full((ROWS, 1, CACHE), 3.0, jnp.float32)], axis=0)
    return (entries * factor).astype(jnp.bfloat16)


def draw_base_cache(key, part):
    return cache_draw(key, (2, ROWS, KVB * HD, CACHE))


def draw_small_cache(key, part):
    return cache_draw(key, (2, 2, ROWS, HS * HD, CACHE))


def draw_base_unembed(key, part):
    key_entries = jax.random.fold_in(key, 0)
    spread = 3.0 / math.sqrt(DB)
    entries = jnp.clip(jax.random.normal(key_entries, (VOCAB, DB), jnp.float32), -6.0, 6.0) * spread
    return entries.astype(jnp.bfloat16)


def draw_lengths(key, part):
    key_values, key_spot = jax.random.split(key, 2)
    drawn = jax.random.randint(key_values, (ROWS,), 1, CACHE + 1)
    longest = jax.random.randint(key_spot, (), 0, ROWS)
    return jnp.where(jnp.arange(ROWS) == longest, CACHE, drawn).astype(jnp.int32)


def place_ends(result, rng, least, largest):
    extent = result.shape
    place = [jax.random.randint(jax.random.fold_in(rng, axis), (), 0, extent[axis]) for axis in range(len(extent))]
    result = result.at[tuple(place)].set(least)
    longest = extent.index(max(extent))
    place[longest] = (place[longest] + 1) % extent[longest]
    return result.at[tuple(place)].set(largest)


def block_levels(key, extent, pieces, least, high):
    gain = 1.0
    for dim, parts in pieces:
        draws = jax.random.uniform(jax.random.fold_in(jax.random.fold_in(key, 6), dim), (parts,), jnp.float32, least / len(pieces), high / len(pieces))
        gain = gain * jnp.repeat(jnp.exp(draws), extent[dim] // parts).reshape((-1,) + (1,) * (len(extent) - 1 - dim))
    return gain


def centred(stream_key, dims, scale, most, cuts=(), kind=jnp.bfloat16):
    values = scale * jax.random.normal(stream_key, dims, jnp.float32)
    if cuts:
        values = values * block_levels(stream_key, dims, cuts, -0.22, 0.18)
    return jnp.clip(values, -most, most).astype(kind)


def setup_inputs(seed: int = 0) -> dict:
    arg_keys = jax.random.split(jax.random.key(seed), 18)
    base_inputs = centred(arg_keys[0], (STEPS, ROWS, DB), 1.0, 6.0, ((1, 2), (2, 16)))
    small_inputs = centred(arg_keys[1], (2, STEPS, ROWS, DS), 1.0, 6.0, ((0, 2), (2, 2), (3, 8)))
    base_norm_gain = jnp.clip(1.0 + 0.18 * jax.random.normal(arg_keys[2], (DB,), jnp.float32), 0.1, 1.9)
    base_query = centred(arg_keys[3], (DB, HB * HD), DB ** -0.5, 0.0625, ((1, 16),))
    base_keys_values = centred(arg_keys[4], (2, DB, KVB * HD), DB ** -0.5, 0.0625, ((2, 16),))
    base_output = centred(arg_keys[5], (HB * HD, DB), (HB * HD) ** -0.5, 0.0625, ((0, 16),))
    base_cache = draw_base_cache(jax.random.fold_in(arg_keys[17], 71), 0)
    base_final_gain = jnp.clip(1.0 + 0.18 * jax.random.normal(arg_keys[7], (DB,), jnp.float32), 0.1, 1.9)
    base_unembed = draw_base_unembed(jax.random.fold_in(arg_keys[17], 71), 0)
    small_norm_gain = jnp.clip(1.0 + 0.18 * jax.random.normal(arg_keys[9], (2, DS), jnp.float32), 0.1, 1.9)
    small_projections = centred(arg_keys[10], (2, 3, DS, HS * HD), DS ** -0.5, 0.09375, ((0, 2), (3, 8)))
    small_output = centred(arg_keys[11], (2, HS * HD, DS), (HS * HD) ** -0.5, 0.09375, ((0, 2), (1, 8)))
    small_cache = draw_small_cache(jax.random.fold_in(arg_keys[17], 71), 0)
    small_final_gain = jnp.clip(1.0 + 0.18 * jax.random.normal(arg_keys[13], (2, DS), jnp.float32), 0.1, 1.9)
    small_unembed = centred(arg_keys[14], (2, 2, VOCAB // 2, DS), (DS // 4) ** -0.5, 0.1875, ((0, 2), (2, 8)))
    lengths = draw_lengths(jax.random.fold_in(arg_keys[17], 71), 0)
    next_tokens = place_ends(jax.random.randint(arg_keys[16], (STEPS, ROWS), 0, VOCAB), jax.random.fold_in(arg_keys[16], 1), 0, VOCAB - 1).astype(jnp.int32)
    return dict(base_inputs=base_inputs, small_inputs=small_inputs, base_norm_gain=base_norm_gain, base_query=base_query, base_keys_values=base_keys_values, base_output=base_output, base_cache=base_cache, base_final_gain=base_final_gain, base_unembed=base_unembed, small_norm_gain=small_norm_gain, small_projections=small_projections, small_output=small_output, small_cache=small_cache, small_final_gain=small_final_gain, small_unembed=small_unembed, lengths=lengths, next_tokens=next_tokens)


EPSILON = 1e-05
NEGATIVE = -1e+30

def rotate_pairs(values, positions, first_pair, head_size):
    pair_count = values.shape[-1] // 2
    pair_index = (first_pair + jnp.arange(pair_count)).astype(jnp.float32)
    frequency = jnp.exp(pair_index * (-2.0 * math.log(10000.0) / head_size))
    angles = positions.astype(jnp.float32)[:, None] * frequency[None, :]
    angles = angles.reshape((values.shape[0],) + (1,) * (values.ndim - 2) + (pair_count,))
    cosine = jnp.cos(angles)
    sine_part = jnp.sin(angles)
    paired = values.reshape(values.shape[:-1] + (pair_count, 2))
    even_part = paired[..., 0]
    odd_part = paired[..., 1]
    turned = jnp.stack([even_part * cosine - odd_part * sine_part, even_part * sine_part + odd_part * cosine], axis=-1)
    return turned.reshape(values.shape)

def norm_rows(values, gain_row):
    values = values.astype(jnp.float32)
    scaling = lax.rsqrt(lax.optimization_barrier(jnp.mean(values * values, axis=-1, keepdims=True)) + EPSILON)
    return (values * scaling * gain_row).astype(jnp.bfloat16)

def attention_weights(cached_scores, fresh_scores, visible, head_size):
    factor = 1.0 / math.sqrt(head_size)
    cached_scores = jnp.where(visible, cached_scores * factor, NEGATIVE)
    fresh_scores = fresh_scores * factor
    row_max = jnp.maximum(lax.optimization_barrier(jnp.max(cached_scores, axis=-1, keepdims=True)), lax.optimization_barrier(jnp.max(fresh_scores, axis=-1, keepdims=True)))
    cached_exp = jnp.exp(cached_scores - row_max)
    fresh_exp = jnp.exp(fresh_scores - row_max)
    totals = lax.optimization_barrier(jnp.sum(cached_exp, axis=-1, keepdims=True)) + lax.optimization_barrier(jnp.sum(fresh_exp, axis=-1, keepdims=True))
    return ((cached_exp / totals).astype(jnp.bfloat16), (fresh_exp / totals).astype(jnp.bfloat16))

def small_model(model_index, small_inputs, lengths, small_norm_gain, small_projections, small_output, small_cache, small_final_gain, small_unembed):
    visible = (jnp.arange(CACHE)[None, :] < lengths[:, None])[:, None, :]
    keys_cached = small_cache[model_index, 0].reshape(ROWS, HS, HD, CACHE).astype(jnp.float32)
    values_cached = small_cache[model_index, 1].reshape(ROWS, HS, HD, CACHE).astype(jnp.float32)
    vocab_table = small_unembed[model_index].reshape(VOCAB, DS)
    new_keys = []
    new_values = []
    logit_steps = []
    for step_index in range(STEPS):
        positions = lengths + step_index
        inputs_now = small_inputs[model_index, step_index]
        normed = norm_rows(inputs_now, small_norm_gain[model_index])
        queries = jnp.dot(normed, small_projections[model_index, 0], preferred_element_type=jnp.float32).reshape(ROWS, HS, HD)
        queries = rotate_pairs(queries, positions, 0, HD).astype(jnp.bfloat16)
        new_key = jnp.dot(normed, small_projections[model_index, 1], preferred_element_type=jnp.float32).reshape(ROWS, HS, HD)
        new_keys.append(rotate_pairs(new_key, positions, 0, HD).astype(jnp.bfloat16))
        new_value = jnp.dot(normed, small_projections[model_index, 2], preferred_element_type=jnp.float32).reshape(ROWS, HS, HD)
        new_values.append(new_value.astype(jnp.bfloat16))
        fresh_keys = jnp.stack(new_keys, axis=-1).astype(jnp.float32)
        fresh_values = jnp.stack(new_values, axis=-1).astype(jnp.float32)
        queries_wide = queries.astype(jnp.float32)
        cached_scores = jnp.einsum('rhd,rhdl->rhl', queries_wide, keys_cached)
        fresh_scores = jnp.einsum('rhd,rhdn->rhn', queries_wide, fresh_keys)
        cached_weights, fresh_weights = attention_weights(cached_scores, fresh_scores, visible, HD)
        head_values = jnp.einsum('rhl,rhdl->rhd', cached_weights.astype(jnp.float32), values_cached)
        head_values = head_values + jnp.einsum('rhn,rhdn->rhd', fresh_weights.astype(jnp.float32), fresh_values)
        head_values = head_values.astype(jnp.bfloat16).reshape(ROWS, HS * HD)
        hidden = inputs_now.astype(jnp.float32) + jnp.dot(head_values, small_output[model_index], preferred_element_type=jnp.float32)
        final_rows = norm_rows(hidden, small_final_gain[model_index])
        logit_steps.append(jnp.dot(final_rows, vocab_table.T, preferred_element_type=jnp.float32))
    return logit_steps

def base_model(base_inputs, lengths, base_norm_gain, base_query, base_keys_values, base_output, base_cache, base_final_gain, base_unembed):
    share_count = N_GRP * N_TP // KVB
    slice_width = HD // share_count
    group_size = HB // KVB
    visible = (jnp.arange(CACHE)[None, :] < lengths[:, None])[:, None, None, :]
    keys_cached = base_cache[0].reshape(ROWS, KVB, HD, CACHE).astype(jnp.float32)
    values_cached = base_cache[1].reshape(ROWS, KVB, HD, CACHE).astype(jnp.float32)
    new_keys = []
    new_values = []
    logit_steps = []
    for step_index in range(STEPS):
        positions = lengths + step_index
        inputs_now = base_inputs[step_index]
        normed = norm_rows(inputs_now, base_norm_gain)
        queries = jnp.dot(normed, base_query, preferred_element_type=jnp.float32)
        queries = queries.reshape(ROWS, KVB, share_count, group_size, slice_width).transpose(0, 1, 3, 2, 4).reshape(ROWS, KVB, group_size, HD)
        queries = rotate_pairs(queries, positions, 0, HD).astype(jnp.bfloat16)
        new_key = jnp.dot(normed, base_keys_values[0], preferred_element_type=jnp.float32).reshape(ROWS, KVB, HD)
        new_keys.append(rotate_pairs(new_key, positions, 0, HD).astype(jnp.bfloat16))
        new_value = jnp.dot(normed, base_keys_values[1], preferred_element_type=jnp.float32).reshape(ROWS, KVB, HD)
        new_values.append(new_value.astype(jnp.bfloat16))
        fresh_keys = jnp.stack(new_keys, axis=-1).astype(jnp.float32)
        fresh_values = jnp.stack(new_values, axis=-1).astype(jnp.float32)
        queries_wide = queries.astype(jnp.float32)
        cached_scores = jnp.einsum('rkgd,rkdl->rkgl', queries_wide, keys_cached)
        fresh_scores = jnp.einsum('rkgd,rkdn->rkgn', queries_wide, fresh_keys)
        cached_weights, fresh_weights = attention_weights(cached_scores, fresh_scores, visible, HD)
        head_values = jnp.einsum('rkgl,rkdl->rkgd', cached_weights.astype(jnp.float32), values_cached)
        head_values = head_values + jnp.einsum('rkgn,rkdn->rkgd', fresh_weights.astype(jnp.float32), fresh_values)
        head_values = head_values.astype(jnp.bfloat16).reshape(ROWS, KVB, group_size, share_count, slice_width)
        head_values = head_values.transpose(0, 1, 3, 2, 4).reshape(ROWS, HB * HD)
        hidden = inputs_now.astype(jnp.float32) + jnp.dot(head_values, base_output, preferred_element_type=jnp.float32)
        final_rows = norm_rows(hidden, base_final_gain)
        logit_steps.append(jnp.dot(final_rows, base_unembed.T, preferred_element_type=jnp.float32))
    return logit_steps

def reference(base_inputs, small_inputs, base_norm_gain, base_query, base_keys_values, base_output, base_cache, base_final_gain, base_unembed, small_norm_gain, small_projections, small_output, small_cache, small_final_gain, small_unembed, lengths, next_tokens):
    expert_steps = small_model(0, small_inputs, lengths, small_norm_gain, small_projections, small_output, small_cache, small_final_gain, small_unembed)
    anti_steps = small_model(1, small_inputs, lengths, small_norm_gain, small_projections, small_output, small_cache, small_final_gain, small_unembed)
    base_steps = base_model(base_inputs, lengths, base_norm_gain, base_query, base_keys_values, base_output, base_cache, base_final_gain, base_unembed)
    log_steps = []
    chosen_total = jnp.zeros((ROWS,), jnp.float32)
    for step_index in range(STEPS):
        steered = base_steps[step_index] + expert_steps[step_index] - anti_steps[step_index]
        row_max = lax.optimization_barrier(jnp.max(steered, axis=-1, keepdims=True))
        log_norm = row_max + jnp.log(lax.optimization_barrier(jnp.sum(jnp.exp(steered - row_max), axis=-1, keepdims=True)))
        step_probs = steered - log_norm
        log_steps.append(step_probs)
        chosen_total = chosen_total + jnp.take_along_axis(step_probs, next_tokens[step_index][:, None].astype(jnp.int32), axis=1)[:, 0]
    return (jnp.stack(log_steps, axis=0), chosen_total)
```

```python
import functools
import math

import jax
import jax.numpy as jnp
from jax import lax
from jax.experimental import pallas as pl
from jax.experimental.pallas import tpu as pltpu
from jax.sharding import PartitionSpec as P

HD = 128
STEPS = 3
CACHE = 128


EPSILON = 1e-05
NEGATIVE = -1e30
VMEM_LIMIT = 60 * 1024 * 1024
LANES = 128


def ring_spot(index, size):
    side = index % 2
    return index // 2 + side * (size - 1 - 2 * (index // 2))


def ring_index(spot, size):
    spot = (spot + 2 * size) % size
    side = spot // (size // 2)
    return 2 * (spot + side * (size - 1 - 2 * spot)) + side


def swap_pairs(values):
    lanes = values.shape[1]
    even = lax.broadcasted_iota(jnp.int32, values.shape, 1) % 2 == 0
    return jnp.where(even, pltpu.roll(values, lanes - 1, 1), pltpu.roll(values, 1, 1))


def square_lanes(x):
    squares = x * x
    total = squares[:, :LANES]
    for start in range(LANES, x.shape[1], LANES):
        total = total + squares[:, start : start + LANES]
    return total


def input_part(
    size,
    greet,
    small_x,
    base_x,
    small_gain,
    base_gain,
    small_w,
    query_w,
    pair_w,
    lengths,
    small_out,
    query_out,
    pair_out,
    small_box,
    base_box,
    small_tiles,
    query_tiles,
    pair_tiles,
    small_total,
    query_total,
    pair_total,
    small_square,
    base_square,
    small_cos,
    small_sin,
    base_cos,
    base_sin,
    local_sems,
    small_w_sems,
    query_w_sems,
    pair_w_sems,
    small_sends,
    small_receives,
    base_sends,
    base_receives,
    core_sends,
    core_receives,
):
    group = lax.axis_index("grp")
    mine = lax.axis_index("tp")
    data = lax.axis_index("dp")
    turn = 1 - 2 * group
    spot = ring_spot(mine, size)
    ahead = (group, ring_index(spot + turn, size), data)
    behind = (group, ring_index(spot - turn, size), data)
    other_core = (1 - group, mine, data)
    rows, small_width = small_x.shape
    base_width = base_x.shape[1]

    def small_source(step):
        return ring_index(spot - step * turn, size)

    def base_source(side, step):
        index = ring_index(spot - (1 - 2 * side) * step * turn, size)
        return (group + side * (1 - 2 * group)) * size + index

    def small_fetch(step):
        rows = pl.ds(pl.multiple_of(small_source(step) * small_width, small_width), small_width)
        return pltpu.make_async_copy(
            small_w.at[0, :, rows, :], small_tiles.at[step], small_w_sems.at[step]
        )

    def query_fetch(side, step):
        rows = pl.ds(pl.multiple_of(base_source(side, step) * base_width, base_width), base_width)
        return pltpu.make_async_copy(
            query_w.at[rows, :], query_tiles.at[side, step], query_w_sems.at[side, step]
        )

    slice_width = pair_w.shape[1]
    copies = LANES // slice_width

    def pair_fetch(side, step, kind, copy):
        columns = pl.ds(pl.multiple_of(base_source(side, step) * base_width, base_width), base_width)
        return pltpu.make_async_copy(
            pair_w.at[kind, :, columns],
            pair_tiles.at[side, step, pl.ds(kind * LANES + copy * slice_width, slice_width)],
            pair_w_sems.at[side, step, kind * copies + copy],
        )

    def pair_fetches(side, step):
        return [pair_fetch(side, step, kind, copy) for kind in range(2) for copy in range(copies)]

    keeps = [
        pltpu.make_async_copy(small_x, small_box.at[0], local_sems.at[0]),
        pltpu.make_async_copy(base_x, base_box.at[0, 0], local_sems.at[1]),
    ]
    for keep in keeps:
        keep.start()

    def fetch_all(step, carry):
        small_fetch(step).start()
        for side in range(2):
            query_fetch(side, step).start()
            for fetch in pair_fetches(side, step):
                fetch.start()
        return carry

    lax.fori_loop(0, size, fetch_all, 0)
    small_total[...] = jnp.zeros_like(small_total)
    query_total[...] = jnp.zeros_like(query_total)
    pair_total[...] = jnp.zeros_like(pair_total)
    small_square[...] = jnp.zeros_like(small_square)
    base_square[...] = jnp.zeros_like(base_square)
    greet()
    for keep in keeps:
        keep.wait()

    half = size // 2

    def hop(box, source, target, sends, receives, device):
        return pltpu.make_async_remote_copy(
            src_ref=box.at[source],
            dst_ref=box.at[target],
            send_sem=sends.at[target],
            recv_sem=receives.at[target],
            device_id=device,
            device_id_type=pl.DeviceIdType.MESH,
        )

    def small_fore(step):
        return hop(small_box, step, step + 1, small_sends, small_receives, ahead)

    def small_back(step):
        source = (size - step) % size
        return hop(small_box, source, size - step - 1, small_sends, small_receives, behind)

    def base_fore(step):
        return hop(base_box.at[0], step, step + 1, base_sends, base_receives, ahead)

    def base_back(step):
        source = (size - step) % size
        return hop(base_box.at[0], source, size - step - 1, base_sends, base_receives, behind)

    def core_hop(step):
        return pltpu.make_async_remote_copy(
            src_ref=base_box.at[0, step],
            dst_ref=base_box.at[1, step],
            send_sem=core_sends.at[step],
            recv_sem=core_receives.at[step],
            device_id=other_core,
            device_id_type=pl.DeviceIdType.MESH,
        )

    def small_work(step):
        small_fetch(step).wait()
        x = small_box[step].astype(jnp.float32)
        small_square[...] += square_lanes(x)
        scaled = (x * small_gain[small_source(step)]).astype(jnp.bfloat16)
        for part in range(small_tiles.shape[1]):
            small_total[part] += jnp.dot(
                scaled, small_tiles[step, part], preferred_element_type=jnp.float32
            )

    def base_work(side, step):
        query_fetch(side, step).wait()
        for fetch in pair_fetches(side, step):
            fetch.wait()
        x = base_box[side, step].astype(jnp.float32)
        base_square[...] += square_lanes(x)
        scaled = (x * base_gain[base_source(side, step)]).astype(jnp.bfloat16)
        query_total[...] += jnp.dot(
            scaled, query_tiles[side, step], preferred_element_type=jnp.float32
        )
        pair_total[...] += lax.dot_general(
            scaled,
            pair_tiles[side, step],
            (((1,), (1,)), ((), ())),
            preferred_element_type=jnp.float32,
        )

    small_fore(0).start()
    small_back(0).start()
    base_fore(0).start()
    base_back(0).start()
    core_hop(0).start()

    def place(row, carry):
        small_cos[pl.ds(row, 1), :] = jnp.full((1, LANES), lengths[row].astype(jnp.float32))
        return carry

    row_count = rows // STEPS
    lax.fori_loop(0, row_count, place, 0)
    start = small_cos[:row_count, :]
    lane = lax.broadcasted_iota(jnp.int32, (1, LANES), 1)
    sign = jnp.where(lane % 2 == 0, -1.0, 1.0)

    def fill_tables(cosine, sine, first_pair, width):
        pair_index = (first_pair + (lane % width) // 2).astype(jnp.float32)
        frequency = jnp.exp(pair_index * (-2.0 * math.log(10000.0) / HD))
        for step in range(STEPS):
            angles = (start + float(step)) * frequency
            piece = slice(step * row_count, (step + 1) * row_count)
            cosine[piece, :] = jnp.cos(angles)
            sine[piece, :] = jnp.sin(angles) * sign

    fill_tables(base_cos, base_sin, mine % copies * (slice_width // 2), slice_width)
    fill_tables(small_cos, small_sin, 0, HD)
    small_work(0)
    base_work(0, 0)

    def ring_step(step, carry):
        small_fore(step - 1).wait_recv()
        small_fore(step).start()
        small_back(step - 1).wait_recv()

        @pl.when(step < half - 1)
        def _():
            small_back(step).start()

        small_work(step)
        small_work(size - step)
        base_fore(step - 1).wait_recv()
        base_fore(step).start()
        base_back(step - 1).wait_recv()

        @pl.when(step < half - 1)
        def _():
            base_back(step).start()

        core_hop(step).start()
        core_hop(size - step).start()
        base_work(0, step)
        base_work(0, size - step)
        core_hop(step - 1).wait_recv()
        base_work(1, step - 1)

        @pl.when(step > 1)
        def _():
            core_hop(size + 1 - step).wait_recv()
            base_work(1, size + 1 - step)

        return carry

    lax.fori_loop(1, half, ring_step, 0)
    core_hop(half - 1).wait_recv()
    base_work(1, half - 1)
    if half > 1:
        core_hop(half + 1).wait_recv()
        base_work(1, half + 1)
    small_fore(half - 1).wait_recv()
    small_work(half)
    base_fore(half - 1).wait_recv()
    core_hop(half).start()
    base_work(0, half)
    core_hop(half).wait_recv()
    base_work(1, half)

    def settle(step, carry):
        small_fore(step).wait_send()
        base_fore(step).wait_send()
        return carry

    def settle_back(step, carry):
        small_back(step).wait_send()
        base_back(step).wait_send()
        return carry

    def settle_core(step, carry):
        core_hop(step).wait_send()
        return carry

    lax.fori_loop(0, half, settle, 0)
    lax.fori_loop(0, half - 1, settle_back, 0)
    lax.fori_loop(0, size, settle_core, 0)

    def scale_of(square_ref, width):
        total = jnp.sum(square_ref[...], axis=-1, keepdims=True)
        return lax.rsqrt(total / width + EPSILON)

    def store(ref, index, values):
        ref[index + (slice(0, rows),)] = values.astype(jnp.bfloat16).astype(jnp.float32)
        rest = ref.shape[-2] - rows
        ref[index + (slice(rows, rows + rest),)] = jnp.zeros((rest, LANES), jnp.float32)

    scale = scale_of(small_square, size * small_width)
    for part in range(small_out.shape[0]):
        for tile in range(small_out.shape[1]):
            columns = slice(tile * LANES, (tile + 1) * LANES)
            values = small_total[part, :, columns] * scale
            if part < 2:
                values = values * small_cos[...] + swap_pairs(values) * small_sin[...]
            store(small_out, (part, tile), values)
    scale = scale_of(base_square, 2 * size * base_width)
    for tile in range(query_out.shape[0]):
        columns = slice(tile * LANES, (tile + 1) * LANES)
        values = query_total[:, columns] * scale
        values = values * base_cos[...] + swap_pairs(values) * base_sin[...]
        store(query_out, (tile,), values)
    values = pair_total[:, :LANES] * scale
    values = values * base_cos[...] + swap_pairs(values) * base_sin[...]
    store(pair_out, (0,), values)
    store(pair_out, (1,), pair_total[:, LANES:] * scale)


def attention_part(
    share,
    begin,
    between,
    small_qkv,
    query,
    pair,
    lengths,
    small_cache,
    base_cache,
    small_out,
    base_out,
    small_keys,
    small_values,
    base_keys,
    base_values,
    small_scores,
    small_fresh,
    small_weights,
    small_fresh_weights,
    base_scores,
    base_stage,
    base_land,
    small_result,
    base_result,
    small_sems,
    base_sems,
    share_sends,
    share_receives,
):
    group = lax.axis_index("grp")
    mine = lax.axis_index("tp")
    data = lax.axis_index("dp")
    row_count = small_keys.shape[0]
    chunk = row_count // small_sems.shape[1]
    chunks = small_sems.shape[1]
    part_rows = small_scores.shape[1]
    base_rows = base_scores.shape[1]
    slice_width = base_cache.shape[2]
    copies = LANES // slice_width
    factor = 1.0 / math.sqrt(HD)
    near = mine - mine % share

    def peer(step):
        return (group, near + (mine % share + step) % share, data)

    def small_fetch(kind, index):
        rows = pl.ds(index * chunk, chunk)
        target = (small_keys, small_values)[kind]
        return pltpu.make_async_copy(
            small_cache.at[0, kind, rows], target.at[rows], small_sems.at[kind, index]
        )

    def base_fetch(kind, copy):
        target = (base_keys, base_values)[kind]
        return pltpu.make_async_copy(
            base_cache.at[kind],
            target.at[:, pl.ds(copy * slice_width, slice_width)],
            base_sems.at[kind, copy],
        )

    for copy in range(copies):
        base_fetch(0, copy).start()
    for kind in range(2):

        def fetch(index, carry, kind=kind):
            small_fetch(kind, index).start()
            return carry

        lax.fori_loop(0, chunks, fetch, 0)
    for copy in range(copies):
        base_fetch(1, copy).start()
    begin()

    def four(ref, row):
        return ref[pl.ds(row, 4, stride=row_count), :]

    def share_copy(step, index):
        rows = pl.ds(index * chunk, chunk)
        return pltpu.make_async_remote_copy(
            src_ref=base_stage.at[rows],
            dst_ref=base_land.at[step - 1, rows],
            send_sem=share_sends.at[step - 1, index],
            recv_sem=share_receives.at[step - 1, index],
            device_id=peer(step),
            device_id_type=pl.DeviceIdType.MESH,
        )

    def nt(x, y):
        return lax.dot_general(x, y, (((1,), (1,)), ((), ())), preferred_element_type=jnp.float32)

    wide = (base_rows, LANES)
    row = lax.broadcasted_iota(jnp.int32, wide, 0)
    lane = lax.broadcasted_iota(jnp.int32, wide, 1)
    base_mask = lane // slice_width == (row // 4) % copies
    step_of = row % 4
    fresh_lanes = [lane // 8 == step_of + odd * (LANES // 16) for odd in range(2)]
    fresh_masks = [
        lanes & (lane % 8 <= step_of) & (lane % 8 < STEPS) for lanes in fresh_lanes
    ]

    for copy in range(copies):
        base_fetch(0, copy).wait()

    def base_left(r):
        tiles = [four(query.at[g // copies], r) for g in range(base_rows // 4)]
        return jnp.where(base_mask, jnp.concatenate(tiles, axis=0), 0.0).astype(jnp.bfloat16)

    def fresh_rows(ref, r):
        both = [[four(ref, r + odd)] * (LANES // 8) for odd in range(2)]
        return jnp.concatenate(both[0] + both[1], axis=0).astype(jnp.bfloat16)

    def base_score(index, carry):
        for inner in range(0, chunk, 2):
            r = index * chunk + inner
            left = jnp.concatenate([base_left(r), base_left(r + 1)], axis=0)
            keys = jnp.concatenate([base_keys[r], base_keys[r + 1]], axis=1)
            both = jnp.dot(left, keys, preferred_element_type=jnp.float32)
            fresh_both = nt(left, fresh_rows(pair.at[0], r))
            for odd in range(2):
                rows = slice(odd * base_rows, (odd + 1) * base_rows)
                scores = both[rows, odd * LANES : (odd + 1) * LANES]
                fresh = jnp.where(fresh_lanes[odd], fresh_both[rows], 0.0)
                moved = pltpu.roll(fresh, 1, 0) + pltpu.roll(fresh, 2, 0) + pltpu.roll(fresh, 3, 0)
                scores = jnp.where(step_of == 3, moved, scores)
                base_scores[r + odd] = scores
                base_stage[r + odd] = scores.astype(base_stage.dtype)
        for step in range(1, share):
            share_copy(step, index).start()
        return carry

    lax.fori_loop(0, chunks, base_score, 0)

    depth = small_keys.shape[1]
    small_row = lax.broadcasted_iota(jnp.int32, (part_rows, depth), 0)
    small_lane = lax.broadcasted_iota(jnp.int32, (part_rows, depth), 1)
    small_mask = small_lane // HD == small_row // 4
    cached_lane = lax.broadcasted_iota(jnp.int32, (part_rows, LANES), 1)
    fresh_step = lax.broadcasted_iota(jnp.int32, (part_rows, 8), 0) % 4
    fresh_index = lax.broadcasted_iota(jnp.int32, (part_rows, 8), 1)
    small_fresh_masks = [
        (fresh_index >= 4 * odd) & (fresh_index <= 4 * odd + fresh_step) & (fresh_index < 4 * odd + STEPS)
        for odd in range(2)
    ]

    def heads_of(part, row, times):
        heads = [four(small_qkv.at[part, head], row) for head in range(depth // HD)]
        heads = [jnp.concatenate([head] * times, axis=0) for head in heads]
        return jnp.concatenate(heads, axis=1)

    def small_left(r):
        left = jnp.where(small_mask, heads_of(0, r, part_rows // 4), 0.0)
        return left.astype(jnp.bfloat16)

    def small_score(index, carry):
        small_fetch(0, index).wait()
        for inner in range(0, chunk, 2):
            r = index * chunk + inner
            left = jnp.concatenate([small_left(r), small_left(r + 1)], axis=0)
            keys = jnp.concatenate([small_keys[r], small_keys[r + 1]], axis=1)
            both = jnp.dot(left, keys, preferred_element_type=jnp.float32)
            fresh_keys = jnp.concatenate([heads_of(1, r, 1), heads_of(1, r + 1, 1)], axis=0)
            fresh = nt(left, fresh_keys.astype(jnp.bfloat16))
            for odd in range(2):
                rows = slice(odd * part_rows, (odd + 1) * part_rows)
                small_scores[r + odd] = both[rows, odd * CACHE : (odd + 1) * CACHE]
                small_fresh[r + odd] = fresh[rows]
        return carry

    lax.fori_loop(0, chunks, small_score, 0)

    def small_softmax(index, carry):
        for inner in range(chunk):
            r = index * chunk + inner
            cached = jnp.where(cached_lane < lengths[r], small_scores[r] * factor, NEGATIVE)
            fresh = jnp.where(small_fresh_masks[inner % 2], small_fresh[r] * factor, NEGATIVE)
            row_max = jnp.maximum(
                jnp.max(cached, axis=-1, keepdims=True), jnp.max(fresh, axis=-1, keepdims=True)
            )
            cached = jnp.exp(cached - row_max)
            fresh = jnp.exp(fresh - row_max)
            total = jnp.sum(cached, axis=-1, keepdims=True) + jnp.sum(
                fresh, axis=-1, keepdims=True
            )
            small_weights[r] = (cached / total).astype(jnp.bfloat16)
            small_fresh_weights[r] = (fresh / total).astype(jnp.bfloat16).astype(jnp.float32)
        return carry

    lax.fori_loop(0, chunks, small_softmax, 0)

    def small_value(index, carry):
        small_fetch(1, index).wait()
        for inner in range(0, chunk, 2):
            r = index * chunk + inner
            none = jnp.zeros((part_rows, CACHE), jnp.bfloat16)
            first = jnp.concatenate([small_weights[r], none], axis=1)
            second = jnp.concatenate([none, small_weights[r + 1]], axis=1)
            left = jnp.concatenate([first, second], axis=0)
            values = jnp.concatenate([small_values[r], small_values[r + 1]], axis=1)
            both = nt(left, values)
            for odd in range(2):
                fresh_values = heads_of(2, r + odd, 1)
                weights = small_fresh_weights[r + odd]
                for head in range(depth // HD):
                    columns = slice(head * HD, (head + 1) * HD)
                    rows = slice(4 * head, 4 * head + 4)
                    total = both[odd * part_rows + 4 * head : odd * part_rows + 4 * head + 4, columns]
                    for n in range(STEPS):
                        total = total + (
                            weights[rows, 4 * odd + n : 4 * odd + n + 1]
                            * fresh_values[n : n + 1, columns]
                        )
                    small_result[head, pl.ds(r + odd, 4, stride=row_count), :] = total
        return carry

    lax.fori_loop(0, chunks, small_value, 0)
    rows = small_out.shape[0]
    for head in range(depth // HD):
        small_out[:, head * HD : (head + 1) * HD] = small_result[head, :rows].astype(small_out.dtype)

    between()
    for copy in range(copies):
        base_fetch(1, copy).wait()

    def base_softmax(r, odd):
        scores = base_scores[r]
        for step in range(share - 1):
            scores = scores + base_land[step, r].astype(jnp.float32)
        fresh = jnp.where(
            step_of == 0,
            pltpu.roll(scores, base_rows - 3, 0),
            jnp.where(
                step_of == 1,
                pltpu.roll(scores, base_rows - 2, 0),
                pltpu.roll(scores, base_rows - 1, 0),
            ),
        )
        cached = jnp.where(lane < lengths[r], scores * factor, NEGATIVE)
        fresh = jnp.where(fresh_masks[odd], fresh * factor, NEGATIVE)
        row_max = jnp.max(jnp.maximum(cached, fresh), axis=-1, keepdims=True)
        cached = jnp.exp(cached - row_max)
        fresh = jnp.exp(fresh - row_max)
        total = jnp.sum(cached + fresh, axis=-1, keepdims=True)
        return (cached / total).astype(jnp.bfloat16), (fresh / total).astype(jnp.bfloat16)

    def base_value(index, carry):
        for step in range(1, share):
            share_copy(step, index).wait_recv()
        for inner in range(0, chunk, 2):
            r = index * chunk + inner
            none = jnp.zeros((base_rows, CACHE), jnp.bfloat16)
            cached, fresh = zip(base_softmax(r, 0), base_softmax(r + 1, 1))
            first = jnp.concatenate([cached[0], none], axis=1)
            second = jnp.concatenate([none, cached[1]], axis=1)
            left = jnp.concatenate([first, second], axis=0)
            values = jnp.concatenate([base_values[r], base_values[r + 1]], axis=1)
            both = nt(left, values) + jnp.dot(
                jnp.concatenate(fresh, axis=0),
                fresh_rows(pair.at[1], r),
                preferred_element_type=jnp.float32,
            )
            for odd in range(2):
                heads = both[odd * base_rows : (odd + 1) * base_rows]
                for tile in range(base_out.shape[1] // LANES):
                    g = tile * copies
                    part = heads[4 * g : 4 * g + 4]
                    for copy in range(1, copies):
                        g = tile * copies + copy
                        part = jnp.where(
                            lane[:4] // slice_width == copy, heads[4 * g : 4 * g + 4], part
                        )
                    base_result[tile, pl.ds(r + odd, 4, stride=row_count), :] = part
        return carry

    lax.fori_loop(0, chunks, base_value, 0)
    for tile in range(base_out.shape[1] // LANES):
        base_out[:, tile * LANES : (tile + 1) * LANES] = base_result[tile, :rows].astype(
            base_out.dtype
        )

    def settle(index, carry):
        for step in range(1, share):
            share_copy(step, index).wait_send()
        return carry

    lax.fori_loop(0, chunks, settle, 0)


def output_part(
    size,
    small_heads,
    base_heads,
    small_gain,
    base_gain,
    next_tokens,
    small_w,
    base_w,
    small_table,
    base_table,
    log_out,
    norm_out,
    chosen_out,
    small_w_tiles,
    base_w_tiles,
    small_stage,
    small_land,
    base_stage,
    base_land,
    core_stage,
    core_land,
    small_box,
    base_box,
    small_logits,
    base_logits,
    theirs,
    small_square,
    base_square,
    stats,
    stats_box,
    tokens,
    small_w_sems,
    base_w_sems,
    small_t_sems,
    base_t_sems,
    sum_sends,
    sum_receives,
    swap_sends,
    swap_receives,
    ring_sends,
    ring_receives,
    core_sends,
    core_receives,
    gap_sems,
    stat_sends,
    stat_receives,
):
    group = lax.axis_index("grp")
    mine = lax.axis_index("tp")
    data = lax.axis_index("dp")
    turn = 1 - 2 * group
    spot = ring_spot(mine, size)
    ahead = (group, ring_index(spot + turn, size), data)
    behind = (group, ring_index(spot - turn, size), data)
    other_core = (1 - group, mine, data)
    place = group * size + mine
    count = 2 * size
    rows, small_width = small_box.shape[1:]
    base_width = base_box.shape[3]
    width = base_table.shape[0]
    row_count = rows // STEPS

    def peer(step):
        index = (place + step) % count
        return (index // size, index % size, data)

    def small_source(step):
        return ring_index(spot - step * turn, size)

    def base_source(side, step):
        index = ring_index(spot - (1 - 2 * side) * step * turn, size)
        return (group + side * (1 - 2 * group)) * size + index

    def columns(block, width):
        return pl.ds(pl.multiple_of(block * width, width), width)

    half = size // 2

    def slot_of(use):
        odd = use % 2
        return odd * ((use + 1) // 2) + (1 - odd) * ((size - use // 2) % size)

    def small_w_fetch(tile):
        return pltpu.make_async_copy(
            small_w.at[0, :, columns(small_source(tile), small_width)],
            small_w_tiles.at[tile],
            small_w_sems.at[tile],
        )

    def base_w_fetch(side, tile):
        return pltpu.make_async_copy(
            base_w.at[:, columns(base_source(side, tile), base_width)],
            base_w_tiles.at[side, tile],
            base_w_sems.at[side, tile],
        )

    def remote(source, target, sends, receives, device):
        return pltpu.make_async_remote_copy(
            src_ref=source,
            dst_ref=target,
            send_sem=sends,
            recv_sem=receives,
            device_id=device,
            device_id_type=pl.DeviceIdType.MESH,
        )

    def sum_hop(model, tile, device):
        stage, land = ((small_stage, small_land), (base_stage, base_land))[model]
        return remote(
            stage.at[tile], land.at[tile], sum_sends.at[model, tile], sum_receives.at[model, tile], device
        )

    def sum_fore(model, step):
        return sum_hop(model, half + step, ahead)

    def sum_back(model, step):
        return sum_hop(model, half - 1 - step, behind)

    def core_sum(tile):
        return remote(
            core_stage.at[tile],
            core_land.at[tile],
            swap_sends.at[tile],
            swap_receives.at[tile],
            other_core,
        )

    def hop(model, source, target, device):
        box = small_box if model == 0 else base_box.at[0]
        return remote(
            box.at[source],
            box.at[target],
            ring_sends.at[model, target],
            ring_receives.at[model, target],
            device,
        )

    def fore(model, step):
        return hop(model, step, step + 1, ahead)

    def back(model, step):
        return hop(model, (size - step) % size, size - step - 1, behind)

    def core_hop(step):
        return remote(
            base_box.at[0, step],
            base_box.at[1, step],
            core_sends.at[step],
            core_receives.at[step],
            other_core,
        )

    def begin():
        def fetch_w(step, carry):
            small_w_fetch(half + step).start()
            small_w_fetch(half - 1 - step).start()
            return carry

        def fetch_base_w(step, carry):
            base_w_fetch(1, half + step).start()
            base_w_fetch(0, half + step).start()
            base_w_fetch(1, half - 1 - step).start()
            base_w_fetch(0, half - 1 - step).start()
            return carry

        lax.fori_loop(0, half, fetch_w, 0)
        lax.fori_loop(0, half, fetch_base_w, 0)
        small_logits[...] = jnp.zeros_like(small_logits)
        base_logits[...] = jnp.zeros_like(base_logits)
        small_square[...] = jnp.zeros_like(small_square)
        base_square[...] = jnp.zeros_like(base_square)

    def small_part(tile):
        small_w_fetch(tile).wait()
        return jnp.dot(small_heads[...], small_w_tiles[tile], preferred_element_type=jnp.float32)

    def base_part(side, tile):
        base_w_fetch(side, tile).wait()
        return jnp.dot(
            base_heads[...], base_w_tiles[side, tile], preferred_element_type=jnp.float32
        )

    def core_send(tile):
        core_stage[tile] = base_part(1, tile).astype(core_stage.dtype)
        core_sum(tile).start()

    def small_send(tile, device, before):
        total = small_part(tile)
        if before is not None:
            sum_hop(0, before, device).wait_recv()
            total = total + small_land[before].astype(jnp.float32)
        small_stage[tile] = total.astype(small_stage.dtype)
        sum_hop(0, tile, device).start()

    def base_send(tile, device, before):
        total = base_part(0, tile)
        core_sum(tile).wait_recv()
        total = total + core_land[tile].astype(jnp.float32)
        if before is not None:
            sum_hop(1, before, device).wait_recv()
            total = total + base_land[before].astype(jnp.float32)
        base_stage[tile] = total.astype(base_stage.dtype)
        sum_hop(1, tile, device).start()

    def start_small():
        small_send(half, ahead, None)
        if half > 1:
            small_send(half - 1, behind, None)

    def rest(small_tiles, base_tiles):
        slots = small_tiles.shape[0]

        def small_fetch(use):
            return pltpu.make_async_copy(
                small_table.at[0, :, :, columns(small_source(slot_of(use)), small_width)],
                small_tiles.at[use % slots],
                small_t_sems.at[use],
            )

        def base_fetch(side, use):
            return pltpu.make_async_copy(
                base_table.at[:, columns(base_source(side, slot_of(use)), base_width)],
                base_tiles.at[side, use % slots],
                base_t_sems.at[side, use],
            )

        for step in range(min(slots, size)):
            small_fetch(step).start()
            base_fetch(0, step).start()
            base_fetch(1, step).start()
        core_send(half)
        if half > 1:
            core_send(half - 1)
        base_send(half, ahead, None)
        if half > 1:
            base_send(half - 1, behind, None)
            core_send(half + 1)
            core_send(half - 2)

        def sum_step(step, carry):
            small_send(half + step, ahead, half + step - 1)
            small_send(half - 1 - step, behind, half - step)
            core_send(half + step + 1)
            core_send(half - 2 - step)
            base_send(half + step, ahead, half + step - 1)
            base_send(half - 1 - step, behind, half - step)
            return carry

        lax.fori_loop(1, half - 1, sum_step, 0)
        last = size - 1
        if half > 1:
            small_send(last, ahead, last - 1)
        total = small_part(0) + small_box[0].astype(jnp.float32)
        if half > 1:
            base_send(last, ahead, last - 1)
        else:
            core_send(0)
        if half > 1:
            sum_hop(0, 1, behind).wait_recv()
            total = total + small_land[1].astype(jnp.float32)
        sum_hop(0, last, ahead).wait_recv()
        total = total + small_land[last].astype(jnp.float32)
        small_box[0] = total.astype(small_box.dtype)
        fore(0, 0).start()
        if half > 1:
            back(0, 0).start()
        total = base_part(0, 0) + base_box[0, 0].astype(jnp.float32)
        core_sum(0).wait_recv()
        total = total + core_land[0].astype(jnp.float32)
        if half > 1:
            sum_hop(1, 1, behind).wait_recv()
            total = total + base_land[1].astype(jnp.float32)
        sum_hop(1, last, ahead).wait_recv()
        total = total + base_land[last].astype(jnp.float32)
        base_box[0, 0] = total.astype(base_box.dtype)
        fore(1, 0).start()
        if half > 1:
            back(1, 0).start()
        core_hop(0).start()

        def place_tokens(row, carry):
            for step in range(STEPS):
                token = next_tokens[step, row] - place * width
                tokens[pl.ds(step * row_count + row, 1), :] = jnp.full((1, LANES), token, jnp.int32)
            return carry

        lax.fori_loop(0, row_count, place_tokens, 0)

        def times(x, table):
            return lax.dot_general(
                x, table, (((1,), (1,)), ((), ())), preferred_element_type=jnp.float32
            )

        def small_work(use):
            small_fetch(use).wait()
            slot = slot_of(use)
            x = small_box[slot].astype(jnp.float32)
            small_square[...] += square_lanes(x)
            scaled = (x * small_gain[small_source(slot)]).astype(jnp.bfloat16)
            for part in range(2):
                small_logits[part] += times(scaled, small_tiles[use % slots, part])

            @pl.when(use + slots < size)
            def _():
                small_fetch(use + slots).start()

        def base_work(side, use):
            base_fetch(side, use).wait()
            slot = slot_of(use)
            x = base_box[side, slot].astype(jnp.float32)
            base_square[...] += square_lanes(x)
            scaled = (x * base_gain[base_source(side, slot)]).astype(jnp.bfloat16)
            base_logits[...] += times(scaled, base_tiles[side, use % slots])

            @pl.when(use + slots < size)
            def _():
                base_fetch(side, use + slots).start()

        small_work(0)
        base_work(0, 0)
        core_hop(0).wait_recv()
        base_work(1, 0)

        def ring_step(step, carry):
            fore(0, step - 1).wait_recv()
            fore(0, step).start()
            back(0, step - 1).wait_recv()

            @pl.when(step < half - 1)
            def _():
                back(0, step).start()

            small_work(2 * step - 1)
            small_work(2 * step)
            fore(1, step - 1).wait_recv()
            fore(1, step).start()
            back(1, step - 1).wait_recv()

            @pl.when(step < half - 1)
            def _():
                back(1, step).start()

            core_hop(step).start()
            core_hop(size - step).start()
            base_work(0, 2 * step - 1)
            base_work(0, 2 * step)
            core_hop(step).wait_recv()
            base_work(1, 2 * step - 1)
            core_hop(size - step).wait_recv()
            base_work(1, 2 * step)
            return carry

        lax.fori_loop(1, half, ring_step, 0)
        fore(0, half - 1).wait_recv()
        small_work(size - 1)

        def scale_of(square_ref, width):
            total = jnp.sum(square_ref[...], axis=-1, keepdims=True)
            return lax.rsqrt(total / width + EPSILON)

        scale = scale_of(small_square, size * small_width)
        for part in range(2):
            small_logits[part] = small_logits[part] * scale
        gap = remote(
            small_logits.at[1 - group], theirs, gap_sems.at[0], gap_sems.at[1], other_core
        )
        gap.start()
        fore(1, half - 1).wait_recv()
        core_hop(half).start()
        base_work(0, size - 1)
        core_hop(half).wait_recv()
        base_work(1, size - 1)
        scale = scale_of(base_square, count * base_width)
        gap.wait_recv()
        sign = turn.astype(jnp.float32)
        steered = base_logits[...] * scale + sign * (small_logits[group] - theirs[...])
        log_out[...] = steered
        row_max = jnp.max(steered, axis=-1, keepdims=True)
        exp_total = jnp.sum(jnp.exp(steered - row_max), axis=-1, keepdims=True)
        lane = lax.broadcasted_iota(jnp.int32, (rows, LANES), 1)
        picked = jnp.zeros((rows, LANES), jnp.float32)
        for start in range(0, width, LANES):
            hit = lane + start == tokens[...]
            picked = picked + jnp.where(hit, log_out[:, start : start + LANES], 0.0)
        picked = jnp.sum(picked, axis=-1, keepdims=True)
        packed = jnp.where(lane == 0, row_max, jnp.where(lane == 1, exp_total, picked))
        stats[...] = jnp.zeros_like(stats)
        stats[:rows] = packed
        turned = stats[...].T
        stats_box[place] = turned[:8]

        def share(step):
            return remote(
                stats_box.at[place],
                stats_box.at[place],
                stat_sends.at[step],
                stat_receives.at[step],
                peer(step),
            )

        def share_start(step, carry):
            share(step).start()
            return carry

        def share_wait(step, carry):
            share(step).wait_recv()
            return carry

        lax.fori_loop(1, count, share_start, 0)
        lax.fori_loop(1, count, share_wait, 0)
        everyone = stats_box[...]
        maxima = everyone[:, 0:1]
        row_max = jnp.max(maxima, axis=0)
        exp_total = jnp.sum(everyone[:, 1:2] * jnp.exp(maxima - row_max[None]), axis=0)
        log_norm = row_max + jnp.log(exp_total)
        chosen = jnp.sum(everyone[:, 2:3], axis=0) - log_norm
        pick = lax.broadcasted_iota(jnp.int32, (LANES, log_norm.shape[1]), 0)
        columns_out = jnp.where(pick == 0, log_norm, chosen).T
        norm_out[...] = columns_out[:rows]
        chosen = columns_out[:row_count]
        for step in range(1, STEPS):
            chosen = chosen + columns_out[step * row_count : (step + 1) * row_count]
        chosen_out[...] = chosen

        def settle(step, carry):
            for model in range(2):
                sum_fore(model, step).wait_send()
                fore(model, step).wait_send()
            return carry

        def settle_back(step, carry):
            for model in range(2):
                sum_back(model, step).wait_send()
                back(model, step).wait_send()
            return carry

        def settle_core(step, carry):
            core_sum(step).wait_send()
            core_hop(step).wait_send()
            return carry

        lax.fori_loop(0, half, settle, 0)
        lax.fori_loop(0, half - 1, settle_back, 0)
        lax.fori_loop(0, size, settle_core, 0)
        gap.wait_send()

        def share_settle(step, carry):
            share(step).wait_send()
            return carry

        lax.fori_loop(1, count, share_settle, 0)

    return begin, start_small, rest


def whole_kernel(
    size,
    share,
    slots,
    small_x,
    base_x,
    small_gain,
    base_gain,
    small_final,
    base_final,
    lengths,
    next_tokens,
    small_w,
    query_w,
    pair_w,
    small_cache,
    base_cache,
    small_out_w,
    base_out_w,
    small_table,
    base_table,
    steered,
    norm,
    chosen,
    small_box,
    base_box,
    small_qkv,
    query,
    pair,
    small_square,
    base_square,
    small_heads,
    base_heads,
    input_sems,
    attention_scratch,
    attention_sems,
    output_scratch,
    output_sems,
):
    group = lax.axis_index("grp")
    mine = lax.axis_index("tp")
    data = lax.axis_index("dp")
    place = group * size + mine
    count = 2 * size
    rows, small_width = small_box.shape[1:]
    base_width = base_box.shape[3]
    row_count, depth = small_cache.shape[2:4]
    parts = small_w.shape[1]
    half = jnp.bfloat16

    def greet():
        barrier = pltpu.get_barrier_semaphore()

        def call(step, carry):
            index = (place + step) % count
            pl.semaphore_signal(
                barrier,
                inc=1,
                device_id=(index // size, index % size, data),
                device_id_type=pl.DeviceIdType.MESH,
            )
            return carry

        lax.fori_loop(1, count, call, 0)
        pl.semaphore_wait(barrier, count - 1)

    def first(small_tiles, query_tiles, pair_tiles, small_total, query_total, pair_total, *tables):
        input_part(
            size,
            greet,
            small_x,
            base_x,
            small_gain,
            base_gain,
            small_w,
            query_w,
            pair_w,
            lengths,
            small_qkv,
            query,
            pair,
            small_box,
            base_box,
            small_tiles,
            query_tiles,
            pair_tiles,
            small_total,
            query_total,
            pair_total,
            small_square,
            base_square,
            *tables,
            *input_sems,
        )

    table = pltpu.VMEM((rows, LANES), jnp.float32)
    pl.run_scoped(
        first,
        pltpu.VMEM((size, parts, small_width, depth), half),
        pltpu.VMEM((2, size, base_width, query_w.shape[1]), half),
        pltpu.VMEM((2, size, 2 * LANES, base_width), half),
        pltpu.VMEM((parts, rows, depth), jnp.float32),
        pltpu.VMEM((rows, query_w.shape[1]), jnp.float32),
        pltpu.VMEM((rows, 2 * LANES), jnp.float32),
        table,
        table,
        table,
        table,
    )
    def after(small_w_tiles, base_w_tiles):
        begin, start_small, rest = output_part(
            size,
            small_heads,
            base_heads,
            small_final,
            base_final,
            next_tokens,
            small_out_w,
            base_out_w,
            small_table,
            base_table,
            steered,
            norm,
            chosen,
            small_w_tiles,
            base_w_tiles,
            *output_scratch[:6],
            small_box,
            base_box,
            *output_scratch[6:9],
            small_square,
            base_square,
            *output_scratch[9:],
            *output_sems,
        )

        def between():
            start_small()

        def second(small_keys, small_values, base_keys, base_values):
            attention_part(
                share,
                begin,
                between,
                small_qkv,
                query,
                pair,
                lengths,
                small_cache,
                base_cache,
                small_heads,
                base_heads,
                small_keys,
                small_values,
                base_keys,
                base_values,
                *attention_scratch,
                *attention_sems,
            )

        cache = pltpu.VMEM((row_count, depth, CACHE), half)
        wide = pltpu.VMEM((row_count, LANES, CACHE), half)
        pl.run_scoped(second, cache, cache, wide, wide)
        vocab = base_table.shape[0]
        pl.run_scoped(
            rest,
            pltpu.VMEM((slots, 2, vocab, small_width), half),
            pltpu.VMEM((2, slots, vocab, base_width), half),
        )

    output_depth = base_out_w.shape[0]
    pl.run_scoped(
        after,
        pltpu.VMEM((size, depth, small_width), half),
        pltpu.VMEM((2, size, output_depth, base_width), half),
    )


def whole_stage(
    small_x,
    base_x,
    small_gain,
    base_gain,
    small_final,
    base_final,
    lengths,
    next_tokens,
    small_w,
    query_w,
    pair_w,
    small_cache,
    base_cache,
    small_out_w,
    base_out_w,
    small_table,
    base_table,
):
    size = lax.axis_size("tp")
    rows, small_width = small_x.shape
    base_width = base_x.shape[1]
    row_count, depth = small_cache.shape[2:4]
    base_depth = query_w.shape[1]
    slice_width = base_cache.shape[2]
    share = HD // slice_width
    copies = LANES // slice_width
    base_rows = 4 * (base_depth // slice_width)
    part_rows = max(8, 4 * (depth // HD))
    chunks = row_count // 8
    parts = small_w.shape[1]
    padded = rows // STEPS * (STEPS + 1)
    vocab = base_table.shape[0]
    stat_rows = rows + -rows % LANES
    slots = 3
    half = jnp.bfloat16
    wide = jnp.float32
    vmem = pl.BlockSpec(memory_space=pltpu.VMEM)
    smem = pl.BlockSpec(memory_space=pltpu.SMEM)
    hbm = pl.BlockSpec(memory_space=pl.ANY)
    dma = pltpu.SemaphoreType.DMA
    space = pltpu.VMEM
    return pl.pallas_call(
        functools.partial(whole_kernel, size, share, slots),
        in_specs=[hbm] * 2 + [vmem] * 4 + [smem] * 2 + [hbm] * 9,
        out_specs=[vmem] * 3,
        out_shape=[
            jax.ShapeDtypeStruct((rows, vocab), wide),
            jax.ShapeDtypeStruct((rows, LANES), wide),
            jax.ShapeDtypeStruct((row_count, LANES), wide),
        ],
        scratch_shapes=[
            space((size, rows, small_width), half),
            space((2, size, rows, base_width), half),
            space((parts, depth // LANES, padded, LANES), wide),
            space((base_depth // LANES, padded, LANES), wide),
            space((2, padded, LANES), wide),
            space((rows, LANES), wide),
            space((rows, LANES), wide),
            space((rows, depth), half),
            space((rows, base_depth), half),
            [dma((2,)), dma((size,)), dma((2, size)), dma((2, size, 2 * copies))]
            + [dma((size,))] * 6,
            [
                space((row_count, part_rows, CACHE), wide),
                space((row_count, part_rows, 8), wide),
                space((row_count, part_rows, CACHE), half),
                space((row_count, part_rows, 8), wide),
                space((row_count, base_rows, CACHE), wide),
                space((row_count, base_rows, CACHE), half),
                space((share - 1, row_count, base_rows, CACHE), half),
                space((depth // LANES, padded, LANES), wide),
                space((base_depth // LANES, padded, LANES), wide),
            ],
            [dma((2, chunks)), dma((2, copies)), dma((share - 1, chunks)), dma((share - 1, chunks))],
            [space((size, rows, small_width), half)] * 2
            + [space((size, rows, base_width), half)] * 4
            + [
                space((2, rows, vocab), wide),
                space((rows, vocab), wide),
                space((rows, vocab), wide),
                space((stat_rows, LANES), wide),
                space((2 * size, 8, stat_rows), wide),
                space((rows, LANES), jnp.int32),
            ],
            [
                dma((size,)),
                dma((2, size)),
                dma((size,)),
                dma((2, size)),
                dma((2, size)),
                dma((2, size)),
                dma((size,)),
                dma((size,)),
                dma((2, size)),
                dma((2, size)),
                dma((size,)),
                dma((size,)),
                dma((2,)),
                dma((2 * size,)),
                dma((2 * size,)),
            ],
        ],
        compiler_params=pltpu.CompilerParams(
            collective_id=0, has_side_effects=True, vmem_limit_bytes=VMEM_LIMIT
        ),
    )(
        small_x,
        base_x,
        small_gain.reshape(size, 1, small_width),
        base_gain.reshape(2 * size, 1, base_width),
        small_final.reshape(size, 1, small_width),
        base_final.reshape(2 * size, 1, base_width),
        lengths,
        next_tokens,
        small_w,
        query_w,
        pair_w,
        small_cache,
        base_cache,
        small_out_w,
        base_out_w,
        small_table,
        base_table,
    )


def finish_kernel(steered, norm, chosen, log_out, chosen_out):
    log_out[...] = steered[...] - norm[:, :1]
    chosen_out[...] = chosen[...].T[1:2]


def finish(steered, norm, chosen):
    whole = pl.BlockSpec(memory_space=pltpu.VMEM)
    return pl.pallas_call(
        finish_kernel,
        in_specs=[whole] * 3,
        out_specs=[whole] * 2,
        out_shape=[
            jax.ShapeDtypeStruct(steered.shape, jnp.float32),
            jax.ShapeDtypeStruct((1, chosen.shape[0]), jnp.float32),
        ],
    )(steered, norm, chosen)


def body(
    base_inputs,
    small_inputs,
    base_norm_gain,
    base_query,
    base_keys_values,
    base_output,
    base_cache,
    base_final_gain,
    base_unembed,
    small_norm_gain,
    small_projections,
    small_output,
    small_cache,
    small_final_gain,
    small_unembed,
    lengths,
    next_tokens,
):
    row_count = lengths.shape[0]
    total_rows = STEPS * row_count
    vocab_width = base_unembed.shape[0]
    small_block = small_inputs.reshape(total_rows, -1)
    base_block = base_inputs.reshape(total_rows, -1)
    pair_weights = jnp.swapaxes(base_keys_values, 1, 2)
    steered, norm, chosen = whole_stage(
        small_block,
        base_block,
        small_norm_gain,
        base_norm_gain,
        small_final_gain,
        base_final_gain,
        lengths,
        next_tokens,
        small_projections,
        base_query,
        pair_weights,
        small_cache,
        base_cache,
        small_output,
        base_output,
        small_unembed,
        base_unembed,
    )
    log_probs, chosen = finish(steered, norm, chosen)
    return log_probs.reshape(STEPS, row_count, vocab_width), chosen.reshape(row_count)


def solution(mesh):
    placed = (
        P(None, "dp", ("grp", "tp")),
        P("grp", None, "dp", "tp"),
        P(),
        P(None, ("grp", "tp")),
        P(None, None, ("grp", "tp")),
        P(("grp", "tp"), None),
        P(None, "dp", ("grp", "tp"), None),
        P(),
        P(("grp", "tp"), None),
        P("grp", None),
        P("grp", None, None, "tp"),
        P("grp", "tp", None),
        P("grp", None, "dp", "tp", None),
        P("grp", None),
        P("grp", None, "tp", None),
        P("dp"),
        P(None, "dp"),
    )
    return jax.shard_map(
        body,
        mesh=mesh,
        in_specs=placed,
        out_specs=(P(None, "dp", ("grp", "tp")), P("dp")),
        check_vma=False,
    )
```

```python
import functools
import math

import jax
import jax.numpy as jnp
from jax import lax
from jax.experimental import pallas as pl
from jax.experimental.pallas import tpu as pltpu
from jax.sharding import PartitionSpec as P

HD = 128
STEPS = 3
CACHE = 128


EPSILON = 1e-05
NEGATIVE = -1e30
VMEM_LIMIT = 61 * 1024 * 1024
LANES = 128


def ring_spot(index, size):
    side = index % 2
    return index // 2 + side * (size - 1 - 2 * (index // 2))


def ring_index(spot, size):
    spot = (spot + 2 * size) % size
    side = spot // (size // 2)
    return 2 * (spot + side * (size - 1 - 2 * spot)) + side


def swap_pairs(values):
    lanes = values.shape[1]
    even = lax.broadcasted_iota(jnp.int32, values.shape, 1) % 2 == 0
    return jnp.where(even, pltpu.roll(values, lanes - 1, 1), pltpu.roll(values, 1, 1))


def square_lanes(x):
    squares = x * x
    total = squares[:, :LANES]
    for start in range(LANES, x.shape[1], LANES):
        total = total + squares[:, start : start + LANES]
    return total


def input_part(
    size,
    greet,
    fetch_keys,
    score,
    small_x,
    base_x,
    small_gain,
    base_gain,
    small_w,
    query_w,
    pair_w,
    lengths,
    small_out,
    query_out,
    pair_out,
    small_box,
    base_box,
    small_tiles,
    query_tiles,
    pair_tiles,
    small_total,
    query_total,
    pair_total,
    small_square,
    base_square,
    small_cos,
    small_sin,
    base_cos,
    base_sin,
    local_sems,
    small_w_sems,
    query_w_sems,
    pair_w_sems,
    small_sends,
    small_receives,
    base_sends,
    base_receives,
    core_sends,
    core_receives,
):
    group = lax.axis_index("grp")
    mine = lax.axis_index("tp")
    data = lax.axis_index("dp")
    turn = 1 - 2 * group
    spot = ring_spot(mine, size)
    ahead = (group, ring_index(spot + turn, size), data)
    behind = (group, ring_index(spot - turn, size), data)
    other_core = (1 - group, mine, data)
    rows, small_width = small_x.shape
    base_width = base_x.shape[1]

    def small_source(step):
        return ring_index(spot - step * turn, size)

    def base_source(side, step):
        index = ring_index(spot - (1 - 2 * side) * step * turn, size)
        return (group + side * (1 - 2 * group)) * size + index

    def small_fetch(step):
        rows = pl.ds(pl.multiple_of(small_source(step) * small_width, small_width), small_width)
        return pltpu.make_async_copy(
            small_w.at[0, :, rows, :], small_tiles.at[step], small_w_sems.at[step]
        )

    def query_fetch(side, step):
        rows = pl.ds(pl.multiple_of(base_source(side, step) * base_width, base_width), base_width)
        return pltpu.make_async_copy(
            query_w.at[rows, :], query_tiles.at[side, step], query_w_sems.at[side, step]
        )

    slice_width = pair_w.shape[1]
    copies = LANES // slice_width

    def pair_fetch(side, step):
        columns = pl.ds(pl.multiple_of(base_source(side, step) * base_width, base_width), base_width)
        return pltpu.make_async_copy(
            pair_w.at[:, :, columns], pair_tiles.at[side, step], pair_w_sems.at[side, step]
        )

    keeps = [
        pltpu.make_async_copy(small_x, small_box.at[0], local_sems.at[0]),
        pltpu.make_async_copy(base_x, base_box.at[0, 0], local_sems.at[1]),
    ]
    for keep in keeps:
        keep.start()

    def fetch_all(step, carry):
        small_fetch(step).start()
        for side in range(2):
            query_fetch(side, step).start()
            pair_fetch(side, step).start()
        return carry

    lax.fori_loop(0, size, fetch_all, 0)
    fetch_keys()
    small_total[...] = jnp.zeros_like(small_total)
    query_total[...] = jnp.zeros_like(query_total)
    pair_total[...] = jnp.zeros_like(pair_total)
    small_square[...] = jnp.zeros_like(small_square)
    base_square[...] = jnp.zeros_like(base_square)
    greet()
    for keep in keeps:
        keep.wait()

    half = size // 2

    def hop(box, source, target, sends, receives, device):
        return pltpu.make_async_remote_copy(
            src_ref=box.at[source],
            dst_ref=box.at[target],
            send_sem=sends.at[target],
            recv_sem=receives.at[target],
            device_id=device,
            device_id_type=pl.DeviceIdType.MESH,
        )

    def small_fore(step):
        return hop(small_box, step, step + 1, small_sends, small_receives, ahead)

    def small_back(step):
        source = (size - step) % size
        return hop(small_box, source, size - step - 1, small_sends, small_receives, behind)

    def base_fore(step):
        return hop(base_box.at[0], step, step + 1, base_sends, base_receives, ahead)

    def base_back(step):
        source = (size - step) % size
        return hop(base_box.at[0], source, size - step - 1, base_sends, base_receives, behind)

    def core_hop(step):
        return pltpu.make_async_remote_copy(
            src_ref=base_box.at[0, step],
            dst_ref=base_box.at[1, step],
            send_sem=core_sends.at[step],
            recv_sem=core_receives.at[step],
            device_id=other_core,
            device_id_type=pl.DeviceIdType.MESH,
        )

    def small_work(step):
        small_fetch(step).wait()
        x = small_box[step].astype(jnp.float32)
        small_square[...] += square_lanes(x)
        scaled = (x * small_gain[small_source(step)]).astype(jnp.bfloat16)
        for part in range(small_tiles.shape[1]):
            small_total[part] += jnp.dot(
                scaled, small_tiles[step, part], preferred_element_type=jnp.float32
            )

    def base_work(side, step):
        query_fetch(side, step).wait()
        pair_fetch(side, step).wait()
        tile = [pair_tiles[side, step, kind] for kind in range(2) for copy in range(copies)]
        x = base_box[side, step].astype(jnp.float32)
        base_square[...] += square_lanes(x)
        scaled = (x * base_gain[base_source(side, step)]).astype(jnp.bfloat16)
        query_total[...] += jnp.dot(
            scaled, query_tiles[side, step], preferred_element_type=jnp.float32
        )
        pair_total[...] += lax.dot_general(
            scaled,
            jnp.concatenate(tile, axis=0),
            (((1,), (1,)), ((), ())),
            preferred_element_type=jnp.float32,
        )

    base_fore(0).start()
    base_back(0).start()
    core_hop(0).start()
    small_fore(0).start()
    small_back(0).start()

    def place(row, carry):
        small_cos[pl.ds(row, 1), :] = jnp.full((1, LANES), lengths[row].astype(jnp.float32))
        return carry

    row_count = rows // STEPS
    lax.fori_loop(0, row_count, place, 0)
    start = small_cos[:row_count, :]
    lane = lax.broadcasted_iota(jnp.int32, (1, LANES), 1)
    sign = jnp.where(lane % 2 == 0, -1.0, 1.0)

    def fill_tables(cosine, sine, first_pair, width):
        pair_index = (first_pair + (lane % width) // 2).astype(jnp.float32)
        frequency = jnp.exp(pair_index * (-2.0 * math.log(10000.0) / HD))
        for step in range(STEPS):
            angles = (start + float(step)) * frequency
            piece = slice(step * row_count, (step + 1) * row_count)
            cosine[piece, :] = jnp.cos(angles)
            sine[piece, :] = jnp.sin(angles) * sign

    fill_tables(base_cos, base_sin, mine % copies * (slice_width // 2), slice_width)
    fill_tables(small_cos, small_sin, 0, HD)
    small_work(0)
    base_work(0, 0)

    def ring_step(step, carry):
        base_fore(step - 1).wait_recv()
        base_fore(step).start()
        base_back(step - 1).wait_recv()

        @pl.when(step < half - 1)
        def _():
            base_back(step).start()

        core_hop(step).start()
        core_hop(size - step).start()
        base_work(0, step)
        base_work(0, size - step)
        small_fore(step - 1).wait_recv()
        small_fore(step).start()
        small_back(step - 1).wait_recv()

        @pl.when(step < half - 1)
        def _():
            small_back(step).start()

        small_work(step)
        small_work(size - step)
        core_hop(step - 1).wait_recv()
        base_work(1, step - 1)

        @pl.when(step > 1)
        def _():
            core_hop(size + 1 - step).wait_recv()
            base_work(1, size + 1 - step)

        return carry

    lax.fori_loop(1, half, ring_step, 0)
    core_hop(half - 1).wait_recv()
    base_work(1, half - 1)
    if half > 1:
        core_hop(half + 1).wait_recv()
        base_work(1, half + 1)
    base_fore(half - 1).wait_recv()
    core_hop(half).start()
    base_work(0, half)
    core_hop(half).wait_recv()
    base_work(1, half)

    def scale_of(square_ref, width):
        total = jnp.sum(square_ref[...], axis=-1, keepdims=True)
        return lax.rsqrt(total / width + EPSILON)

    def store(ref, index, values):
        ref[index + (slice(0, rows),)] = values.astype(jnp.bfloat16).astype(jnp.float32)
        rest = ref.shape[-2] - rows
        ref[index + (slice(rows, rows + rest),)] = jnp.zeros((rest, LANES), jnp.float32)

    scale = scale_of(base_square, 2 * size * base_width)
    for tile in range(query_out.shape[0]):
        columns = slice(tile * LANES, (tile + 1) * LANES)
        values = query_total[:, columns] * scale
        values = values * base_cos[...] + swap_pairs(values) * base_sin[...]
        store(query_out, (tile,), values)
    values = pair_total[:, :LANES] * scale
    values = values * base_cos[...] + swap_pairs(values) * base_sin[...]
    store(pair_out, (0,), values)
    store(pair_out, (1,), pair_total[:, LANES:] * scale)
    score()
    small_fore(half - 1).wait_recv()
    small_work(half)
    scale = scale_of(small_square, size * small_width)
    for part in range(small_out.shape[0]):
        for tile in range(small_out.shape[1]):
            columns = slice(tile * LANES, (tile + 1) * LANES)
            values = small_total[part, :, columns] * scale
            if part < 2:
                values = values * small_cos[...] + swap_pairs(values) * small_sin[...]
            store(small_out, (part, tile), values)

    def settle(step, carry):
        small_fore(step).wait_send()
        base_fore(step).wait_send()
        return carry

    def settle_back(step, carry):
        small_back(step).wait_send()
        base_back(step).wait_send()
        return carry

    def settle_core(step, carry):
        core_hop(step).wait_send()
        return carry

    lax.fori_loop(0, half, settle, 0)
    lax.fori_loop(0, half - 1, settle_back, 0)
    lax.fori_loop(0, size, settle_core, 0)


def attention_part(
    share,
    small_qkv,
    query,
    pair,
    lengths,
    small_cache,
    base_cache,
    small_out,
    base_out,
    small_keys,
    base_keys,
    small_scores,
    small_fresh,
    small_weights,
    small_fresh_weights,
    base_scores,
    base_stage,
    base_land,
    small_result,
    base_result,
    small_sems,
    base_sems,
    share_sends,
    share_receives,
):
    group = lax.axis_index("grp")
    mine = lax.axis_index("tp")
    data = lax.axis_index("dp")
    row_count = small_keys.shape[0]
    chunk = row_count // small_sems.shape[1]
    chunks = small_sems.shape[1]
    part_rows = small_scores.shape[1]
    base_rows = base_scores.shape[1]
    slice_width = base_cache.shape[2]
    copies = LANES // slice_width
    factor = 1.0 / math.sqrt(HD)
    near = mine - mine % share

    def peer(step):
        return (group, near + (mine % share + step) % share, data)

    def small_fetch(kind, index, target):
        rows = pl.ds(index * chunk, chunk)
        return pltpu.make_async_copy(
            small_cache.at[0, kind, rows], target.at[rows], small_sems.at[kind, index]
        )

    def base_fetch(kind, copy, target):
        return pltpu.make_async_copy(
            base_cache.at[kind],
            target.at[:, pl.ds(copy * slice_width, slice_width)],
            base_sems.at[kind, copy],
        )

    def fetch_small(kind, target):
        def fetch(index, carry):
            small_fetch(kind, index, target).start()
            return carry

        lax.fori_loop(0, chunks, fetch, 0)

    def fetch_keys():
        for copy in range(copies):
            base_fetch(0, copy, base_keys).start()
        fetch_small(0, small_keys)

    def four(ref, row):
        return ref[pl.ds(row, 4, stride=row_count), :]

    def share_copy(step, index):
        rows = pl.ds(index * chunk, chunk)
        return pltpu.make_async_remote_copy(
            src_ref=base_stage.at[rows],
            dst_ref=base_land.at[step - 1, rows],
            send_sem=share_sends.at[step - 1, index],
            recv_sem=share_receives.at[step - 1, index],
            device_id=peer(step),
            device_id_type=pl.DeviceIdType.MESH,
        )

    def nt(x, y):
        return lax.dot_general(x, y, (((1,), (1,)), ((), ())), preferred_element_type=jnp.float32)

    wide = (base_rows, LANES)
    row = lax.broadcasted_iota(jnp.int32, wide, 0)
    lane = lax.broadcasted_iota(jnp.int32, wide, 1)
    base_mask = lane // slice_width == (row // 4) % copies
    step_of = row % 4
    fresh_lanes = [lane // 8 == step_of + odd * (LANES // 16) for odd in range(2)]
    fresh_masks = [
        lanes & (lane % 8 <= step_of) & (lane % 8 < STEPS) for lanes in fresh_lanes
    ]

    def base_left(r):
        tiles = [four(query.at[g // copies], r) for g in range(base_rows // 4)]
        return jnp.where(base_mask, jnp.concatenate(tiles, axis=0), 0.0).astype(jnp.bfloat16)

    def fresh_rows(ref, r):
        both = [[four(ref, r + odd)] * (LANES // 8) for odd in range(2)]
        return jnp.concatenate(both[0] + both[1], axis=0).astype(jnp.bfloat16)

    def base_score(index, carry):
        for inner in range(0, chunk, 2):
            r = index * chunk + inner
            left = jnp.concatenate([base_left(r), base_left(r + 1)], axis=0)
            keys = jnp.concatenate([base_keys[r], base_keys[r + 1]], axis=1)
            both = jnp.dot(left, keys, preferred_element_type=jnp.float32)
            fresh_both = nt(left, fresh_rows(pair.at[0], r))
            for odd in range(2):
                rows = slice(odd * base_rows, (odd + 1) * base_rows)
                scores = both[rows, odd * LANES : (odd + 1) * LANES]
                fresh = jnp.where(fresh_lanes[odd], fresh_both[rows], 0.0)
                moved = pltpu.roll(fresh, 1, 0) + pltpu.roll(fresh, 2, 0) + pltpu.roll(fresh, 3, 0)
                scores = jnp.where(step_of == 3, moved, scores)
                base_scores[r + odd] = scores
                base_stage[r + odd] = scores.astype(base_stage.dtype)
        for step in range(1, share):
            share_copy(step, index).start()
        return carry


    depth = small_keys.shape[1]
    small_row = lax.broadcasted_iota(jnp.int32, (part_rows, depth), 0)
    small_lane = lax.broadcasted_iota(jnp.int32, (part_rows, depth), 1)
    small_mask = small_lane // HD == small_row // 4
    cached_lane = lax.broadcasted_iota(jnp.int32, (part_rows, LANES), 1)
    fresh_step = lax.broadcasted_iota(jnp.int32, (part_rows, 8), 0) % 4
    fresh_index = lax.broadcasted_iota(jnp.int32, (part_rows, 8), 1)
    small_fresh_masks = [
        (fresh_index >= 4 * odd) & (fresh_index <= 4 * odd + fresh_step) & (fresh_index < 4 * odd + STEPS)
        for odd in range(2)
    ]

    def heads_of(part, row, times):
        heads = [four(small_qkv.at[part, head], row) for head in range(depth // HD)]
        heads = [jnp.concatenate([head] * times, axis=0) for head in heads]
        return jnp.concatenate(heads, axis=1)

    def small_left(r):
        left = jnp.where(small_mask, heads_of(0, r, part_rows // 4), 0.0)
        return left.astype(jnp.bfloat16)

    def small_score(index, carry):
        small_fetch(0, index, small_keys).wait()
        for inner in range(0, chunk, 2):
            r = index * chunk + inner
            left = jnp.concatenate([small_left(r), small_left(r + 1)], axis=0)
            keys = jnp.concatenate([small_keys[r], small_keys[r + 1]], axis=1)
            both = jnp.dot(left, keys, preferred_element_type=jnp.float32)
            fresh_keys = jnp.concatenate([heads_of(1, r, 1), heads_of(1, r + 1, 1)], axis=0)
            fresh = nt(left, fresh_keys.astype(jnp.bfloat16))
            for odd in range(2):
                rows = slice(odd * part_rows, (odd + 1) * part_rows)
                small_scores[r + odd] = both[rows, odd * CACHE : (odd + 1) * CACHE]
                small_fresh[r + odd] = fresh[rows]
        return carry

    def score():
        for copy in range(copies):
            base_fetch(0, copy, base_keys).wait()
        lax.fori_loop(0, chunks, base_score, 0)

    def small_softmax(index, carry):
        for inner in range(chunk):
            r = index * chunk + inner
            cached = jnp.where(cached_lane < lengths[r], small_scores[r] * factor, NEGATIVE)
            fresh = jnp.where(small_fresh_masks[inner % 2], small_fresh[r] * factor, NEGATIVE)
            row_max = jnp.maximum(
                jnp.max(cached, axis=-1, keepdims=True), jnp.max(fresh, axis=-1, keepdims=True)
            )
            cached = jnp.exp(cached - row_max)
            fresh = jnp.exp(fresh - row_max)
            total = jnp.sum(cached, axis=-1, keepdims=True) + jnp.sum(
                fresh, axis=-1, keepdims=True
            )
            small_weights[r] = (cached / total).astype(jnp.bfloat16)
            small_fresh_weights[r] = (fresh / total).astype(jnp.bfloat16).astype(jnp.float32)
        return carry


    def finish(begin, between, small_values, base_values):
        fetch_small(1, small_values)
        for copy in range(copies):
            base_fetch(1, copy, base_values).start()
        begin()
        lax.fori_loop(0, chunks, small_score, 0)
        lax.fori_loop(0, chunks, small_softmax, 0)

        def small_value(index, carry):
            small_fetch(1, index, small_values).wait()
            for inner in range(0, chunk, 2):
                r = index * chunk + inner
                none = jnp.zeros((part_rows, CACHE), jnp.bfloat16)
                first = jnp.concatenate([small_weights[r], none], axis=1)
                second = jnp.concatenate([none, small_weights[r + 1]], axis=1)
                left = jnp.concatenate([first, second], axis=0)
                values = jnp.concatenate([small_values[r], small_values[r + 1]], axis=1)
                both = nt(left, values)
                for odd in range(2):
                    fresh_values = heads_of(2, r + odd, 1)
                    weights = small_fresh_weights[r + odd]
                    for head in range(depth // HD):
                        columns = slice(head * HD, (head + 1) * HD)
                        rows = slice(4 * head, 4 * head + 4)
                        total = both[odd * part_rows + 4 * head : odd * part_rows + 4 * head + 4, columns]
                        for n in range(STEPS):
                            total = total + (
                                weights[rows, 4 * odd + n : 4 * odd + n + 1]
                                * fresh_values[n : n + 1, columns]
                            )
                        small_result[head, pl.ds(r + odd, 4, stride=row_count), :] = total
            return carry

        lax.fori_loop(0, chunks, small_value, 0)
        rows = small_out.shape[0]
        for head in range(depth // HD):
            small_out[:, head * HD : (head + 1) * HD] = small_result[head, :rows].astype(small_out.dtype)

        between()
        for copy in range(copies):
            base_fetch(1, copy, base_values).wait()

        def base_softmax(r, odd):
            scores = base_scores[r]
            for step in range(share - 1):
                scores = scores + base_land[step, r].astype(jnp.float32)
            fresh = jnp.where(
                step_of == 0,
                pltpu.roll(scores, base_rows - 3, 0),
                jnp.where(
                    step_of == 1,
                    pltpu.roll(scores, base_rows - 2, 0),
                    pltpu.roll(scores, base_rows - 1, 0),
                ),
            )
            cached = jnp.where(lane < lengths[r], scores * factor, NEGATIVE)
            fresh = jnp.where(fresh_masks[odd], fresh * factor, NEGATIVE)
            row_max = jnp.max(jnp.maximum(cached, fresh), axis=-1, keepdims=True)
            cached = jnp.exp(cached - row_max)
            fresh = jnp.exp(fresh - row_max)
            total = jnp.sum(cached + fresh, axis=-1, keepdims=True)
            return (cached / total).astype(jnp.bfloat16), (fresh / total).astype(jnp.bfloat16)

        def base_value(index, carry):
            for step in range(1, share):
                share_copy(step, index).wait_recv()
            for inner in range(0, chunk, 2):
                r = index * chunk + inner
                none = jnp.zeros((base_rows, CACHE), jnp.bfloat16)
                cached, fresh = zip(base_softmax(r, 0), base_softmax(r + 1, 1))
                first = jnp.concatenate([cached[0], none], axis=1)
                second = jnp.concatenate([none, cached[1]], axis=1)
                left = jnp.concatenate([first, second], axis=0)
                values = jnp.concatenate([base_values[r], base_values[r + 1]], axis=1)
                both = nt(left, values) + jnp.dot(
                    jnp.concatenate(fresh, axis=0),
                    fresh_rows(pair.at[1], r),
                    preferred_element_type=jnp.float32,
                )
                for odd in range(2):
                    heads = both[odd * base_rows : (odd + 1) * base_rows]
                    for tile in range(base_out.shape[1] // LANES):
                        g = tile * copies
                        part = heads[4 * g : 4 * g + 4]
                        for copy in range(1, copies):
                            g = tile * copies + copy
                            part = jnp.where(
                                lane[:4] // slice_width == copy, heads[4 * g : 4 * g + 4], part
                            )
                        base_result[tile, pl.ds(r + odd, 4, stride=row_count), :] = part
            return carry

        lax.fori_loop(0, chunks, base_value, 0)
        for tile in range(base_out.shape[1] // LANES):
            base_out[:, tile * LANES : (tile + 1) * LANES] = base_result[tile, :rows].astype(
                base_out.dtype
            )

        def settle(index, carry):
            for step in range(1, share):
                share_copy(step, index).wait_send()
            return carry

        lax.fori_loop(0, chunks, settle, 0)

    return fetch_keys, score, finish


def output_part(
    size,
    small_heads,
    base_heads,
    small_gain,
    base_gain,
    next_tokens,
    small_w,
    base_w,
    small_table,
    base_table,
    log_out,
    norm_out,
    chosen_out,
    small_w_tiles,
    base_w_tiles,
    small_stage,
    small_land,
    base_stage,
    base_land,
    core_stage,
    core_land,
    small_box,
    base_box,
    small_logits,
    base_logits,
    theirs,
    small_square,
    base_square,
    stats,
    stats_box,
    tokens,
    small_w_sems,
    base_w_sems,
    small_t_sems,
    base_t_sems,
    sum_sends,
    sum_receives,
    swap_sends,
    swap_receives,
    ring_sends,
    ring_receives,
    core_sends,
    core_receives,
    gap_sems,
    stat_sends,
    stat_receives,
):
    group = lax.axis_index("grp")
    mine = lax.axis_index("tp")
    data = lax.axis_index("dp")
    turn = 1 - 2 * group
    spot = ring_spot(mine, size)
    ahead = (group, ring_index(spot + turn, size), data)
    behind = (group, ring_index(spot - turn, size), data)
    other_core = (1 - group, mine, data)
    place = group * size + mine
    count = 2 * size
    rows, small_width = small_box.shape[1:]
    base_width = base_box.shape[3]
    width = base_table.shape[0]
    row_count = rows // STEPS

    def peer(step):
        index = (place + step) % count
        return (index // size, index % size, data)

    def small_source(step):
        return ring_index(spot - step * turn, size)

    def base_source(side, step):
        index = ring_index(spot - (1 - 2 * side) * step * turn, size)
        return (group + side * (1 - 2 * group)) * size + index

    def columns(block, width):
        return pl.ds(pl.multiple_of(block * width, width), width)

    half = size // 2

    def slot_of(use):
        odd = use % 2
        return odd * ((use + 1) // 2) + (1 - odd) * ((size - use // 2) % size)

    def small_w_fetch(tile):
        return pltpu.make_async_copy(
            small_w.at[0, :, columns(small_source(tile), small_width)],
            small_w_tiles.at[tile],
            small_w_sems.at[tile],
        )

    def base_w_fetch(side, tile):
        return pltpu.make_async_copy(
            base_w.at[:, columns(base_source(side, tile), base_width)],
            base_w_tiles.at[side, tile],
            base_w_sems.at[side, tile],
        )

    def remote(source, target, sends, receives, device):
        return pltpu.make_async_remote_copy(
            src_ref=source,
            dst_ref=target,
            send_sem=sends,
            recv_sem=receives,
            device_id=device,
            device_id_type=pl.DeviceIdType.MESH,
        )

    def sum_hop(model, tile, device):
        stage, land = ((small_stage, small_land), (base_stage, base_land))[model]
        return remote(
            stage.at[tile], land.at[tile], sum_sends.at[model, tile], sum_receives.at[model, tile], device
        )

    def sum_fore(model, step):
        return sum_hop(model, half + step, ahead)

    def sum_back(model, step):
        return sum_hop(model, half - 1 - step, behind)

    def core_sum(tile):
        return remote(
            core_stage.at[tile],
            core_land.at[tile],
            swap_sends.at[tile],
            swap_receives.at[tile],
            other_core,
        )

    def hop(model, source, target, device):
        box = small_box if model == 0 else base_box.at[0]
        return remote(
            box.at[source],
            box.at[target],
            ring_sends.at[model, target],
            ring_receives.at[model, target],
            device,
        )

    def fore(model, step):
        return hop(model, step, step + 1, ahead)

    def back(model, step):
        return hop(model, (size - step) % size, size - step - 1, behind)

    def core_hop(step):
        return remote(
            base_box.at[0, step],
            base_box.at[1, step],
            core_sends.at[step],
            core_receives.at[step],
            other_core,
        )

    def begin():
        def fetch_w(step, carry):
            small_w_fetch(half + step).start()
            small_w_fetch(half - 1 - step).start()
            return carry

        def fetch_base_w(step, carry):
            base_w_fetch(1, half + step).start()
            base_w_fetch(0, half + step).start()
            base_w_fetch(1, half - 1 - step).start()
            base_w_fetch(0, half - 1 - step).start()
            return carry

        lax.fori_loop(0, half, fetch_w, 0)
        lax.fori_loop(0, half, fetch_base_w, 0)
        small_logits[...] = jnp.zeros_like(small_logits)
        base_logits[...] = jnp.zeros_like(base_logits)
        small_square[...] = jnp.zeros_like(small_square)
        base_square[...] = jnp.zeros_like(base_square)

    def small_part(tile):
        small_w_fetch(tile).wait()
        return jnp.dot(small_heads[...], small_w_tiles[tile], preferred_element_type=jnp.float32)

    def base_part(side, tile):
        base_w_fetch(side, tile).wait()
        return jnp.dot(
            base_heads[...], base_w_tiles[side, tile], preferred_element_type=jnp.float32
        )

    def core_send(tile):
        core_stage[tile] = base_part(1, tile).astype(core_stage.dtype)
        core_sum(tile).start()

    def small_send(tile, device, before):
        total = small_part(tile)
        if before is not None:
            sum_hop(0, before, device).wait_recv()
            total = total + small_land[before].astype(jnp.float32)
        small_stage[tile] = total.astype(small_stage.dtype)
        sum_hop(0, tile, device).start()

    def base_send(tile, device, before):
        total = base_part(0, tile)
        core_sum(tile).wait_recv()
        total = total + core_land[tile].astype(jnp.float32)
        if before is not None:
            sum_hop(1, before, device).wait_recv()
            total = total + base_land[before].astype(jnp.float32)
        base_stage[tile] = total.astype(base_stage.dtype)
        sum_hop(1, tile, device).start()

    def start_small():
        small_send(half, ahead, None)
        if half > 1:
            small_send(half - 1, behind, None)

    def rest(small_tiles, base_tiles):
        slots = small_tiles.shape[0]

        def small_fetch(use):
            return pltpu.make_async_copy(
                small_table.at[0, :, :, columns(small_source(slot_of(use)), small_width)],
                small_tiles.at[use % slots],
                small_t_sems.at[use],
            )

        def base_fetch(side, use):
            return pltpu.make_async_copy(
                base_table.at[:, columns(base_source(side, slot_of(use)), base_width)],
                base_tiles.at[side, use % slots],
                base_t_sems.at[side, use],
            )

        core_send(half)
        if half > 1:
            core_send(half - 1)
        base_send(half, ahead, None)
        if half > 1:
            base_send(half - 1, behind, None)
            core_send(half + 1)
            core_send(half - 2)
        for step in range(min(slots, size)):
            small_fetch(step).start()
            base_fetch(0, step).start()
            base_fetch(1, step).start()

        def sum_step(step, carry):
            small_send(half + step, ahead, half + step - 1)
            small_send(half - 1 - step, behind, half - step)
            core_send(half + step + 1)
            core_send(half - 2 - step)
            base_send(half + step, ahead, half + step - 1)
            base_send(half - 1 - step, behind, half - step)
            return carry

        lax.fori_loop(1, half - 1, sum_step, 0)
        last = size - 1
        if half > 1:
            small_send(last, ahead, last - 1)
        total = small_part(0) + small_box[0].astype(jnp.float32)
        if half > 1:
            base_send(last, ahead, last - 1)
        else:
            core_send(0)
        if half > 1:
            sum_hop(0, 1, behind).wait_recv()
            total = total + small_land[1].astype(jnp.float32)
        sum_hop(0, last, ahead).wait_recv()
        total = total + small_land[last].astype(jnp.float32)
        small_box[0] = total.astype(small_box.dtype)
        fore(0, 0).start()
        if half > 1:
            back(0, 0).start()
        total = base_part(0, 0) + base_box[0, 0].astype(jnp.float32)
        core_sum(0).wait_recv()
        total = total + core_land[0].astype(jnp.float32)
        if half > 1:
            sum_hop(1, 1, behind).wait_recv()
            total = total + base_land[1].astype(jnp.float32)
        sum_hop(1, last, ahead).wait_recv()
        total = total + base_land[last].astype(jnp.float32)
        base_box[0, 0] = total.astype(base_box.dtype)
        fore(1, 0).start()
        if half > 1:
            back(1, 0).start()
        core_hop(0).start()

        def place_tokens(row, carry):
            for step in range(STEPS):
                token = next_tokens[step, row] - place * width
                tokens[pl.ds(step * row_count + row, 1), :] = jnp.full((1, LANES), token, jnp.int32)
            return carry

        lax.fori_loop(0, row_count, place_tokens, 0)

        def times(x, table):
            return lax.dot_general(
                x, table, (((1,), (1,)), ((), ())), preferred_element_type=jnp.float32
            )

        def small_work(use):
            small_fetch(use).wait()
            slot = slot_of(use)
            x = small_box[slot].astype(jnp.float32)
            small_square[...] += square_lanes(x)
            scaled = (x * small_gain[small_source(slot)]).astype(jnp.bfloat16)
            for part in range(2):
                small_logits[part] += times(scaled, small_tiles[use % slots, part])

            @pl.when(use + slots < size)
            def _():
                small_fetch(use + slots).start()

        def base_work(side, use):
            base_fetch(side, use).wait()
            slot = slot_of(use)
            x = base_box[side, slot].astype(jnp.float32)
            base_square[...] += square_lanes(x)
            scaled = (x * base_gain[base_source(side, slot)]).astype(jnp.bfloat16)
            base_logits[...] += times(scaled, base_tiles[side, use % slots])

            @pl.when(use + slots < size)
            def _():
                base_fetch(side, use + slots).start()

        small_work(0)
        base_work(0, 0)
        core_hop(0).wait_recv()
        base_work(1, 0)

        def ring_step(step, carry):
            fore(0, step - 1).wait_recv()
            fore(0, step).start()
            back(0, step - 1).wait_recv()

            @pl.when(step < half - 1)
            def _():
                back(0, step).start()

            small_work(2 * step - 1)
            small_work(2 * step)
            fore(1, step - 1).wait_recv()
            fore(1, step).start()
            back(1, step - 1).wait_recv()

            @pl.when(step < half - 1)
            def _():
                back(1, step).start()

            core_hop(step).start()
            core_hop(size - step).start()
            base_work(0, 2 * step - 1)
            base_work(0, 2 * step)
            core_hop(step).wait_recv()
            base_work(1, 2 * step - 1)
            core_hop(size - step).wait_recv()
            base_work(1, 2 * step)
            return carry

        lax.fori_loop(1, half, ring_step, 0)
        fore(0, half - 1).wait_recv()
        small_work(size - 1)

        def scale_of(square_ref, width):
            total = jnp.sum(square_ref[...], axis=-1, keepdims=True)
            return lax.rsqrt(total / width + EPSILON)

        scale = scale_of(small_square, size * small_width)
        for part in range(2):
            small_logits[part] = small_logits[part] * scale
        gap = remote(
            small_logits.at[1 - group], theirs, gap_sems.at[0], gap_sems.at[1], other_core
        )
        gap.start()
        fore(1, half - 1).wait_recv()
        core_hop(half).start()
        base_work(0, size - 1)
        core_hop(half).wait_recv()
        base_work(1, size - 1)
        scale = scale_of(base_square, count * base_width)
        gap.wait_recv()
        sign = turn.astype(jnp.float32)
        steered = base_logits[...] * scale + sign * (small_logits[group] - theirs[...])
        log_out[...] = steered
        row_max = jnp.max(steered, axis=-1, keepdims=True)
        exp_total = jnp.sum(jnp.exp(steered - row_max), axis=-1, keepdims=True)
        lane = lax.broadcasted_iota(jnp.int32, (rows, LANES), 1)
        picked = jnp.zeros((rows, LANES), jnp.float32)
        for start in range(0, width, LANES):
            hit = lane + start == tokens[...]
            picked = picked + jnp.where(hit, log_out[:, start : start + LANES], 0.0)
        picked = jnp.sum(picked, axis=-1, keepdims=True)
        packed = jnp.where(lane == 0, row_max, jnp.where(lane == 1, exp_total, picked))
        stats[...] = jnp.zeros_like(stats)
        stats[:rows] = packed
        turned = stats[...].T
        stats_box[place] = turned[:8]

        def share(step):
            return remote(
                stats_box.at[place],
                stats_box.at[place],
                stat_sends.at[step],
                stat_receives.at[step],
                peer(step),
            )

        def share_start(step, carry):
            share(step).start()
            return carry

        def share_wait(step, carry):
            share(step).wait_recv()
            return carry

        lax.fori_loop(1, count, share_start, 0)
        lax.fori_loop(1, count, share_wait, 0)
        everyone = stats_box[...]
        maxima = everyone[:, 0:1]
        row_max = jnp.max(maxima, axis=0)
        exp_total = jnp.sum(everyone[:, 1:2] * jnp.exp(maxima - row_max[None]), axis=0)
        log_norm = row_max + jnp.log(exp_total)
        chosen = jnp.sum(everyone[:, 2:3], axis=0) - log_norm
        pick = lax.broadcasted_iota(jnp.int32, (LANES, log_norm.shape[1]), 0)
        columns_out = jnp.where(pick == 0, log_norm, chosen).T
        norm_out[...] = columns_out[:rows]
        chosen = columns_out[:row_count]
        for step in range(1, STEPS):
            chosen = chosen + columns_out[step * row_count : (step + 1) * row_count]
        chosen_out[...] = chosen

        def settle(step, carry):
            for model in range(2):
                sum_fore(model, step).wait_send()
                fore(model, step).wait_send()
            return carry

        def settle_back(step, carry):
            for model in range(2):
                sum_back(model, step).wait_send()
                back(model, step).wait_send()
            return carry

        def settle_core(step, carry):
            core_sum(step).wait_send()
            core_hop(step).wait_send()
            return carry

        lax.fori_loop(0, half, settle, 0)
        lax.fori_loop(0, half - 1, settle_back, 0)
        lax.fori_loop(0, size, settle_core, 0)
        gap.wait_send()

        def share_settle(step, carry):
            share(step).wait_send()
            return carry

        lax.fori_loop(1, count, share_settle, 0)

    return begin, start_small, rest


def whole_kernel(
    size,
    share,
    slots,
    small_x,
    base_x,
    small_gain,
    base_gain,
    small_final,
    base_final,
    lengths,
    next_tokens,
    small_w,
    query_w,
    pair_w,
    small_cache,
    base_cache,
    small_out_w,
    base_out_w,
    small_table,
    base_table,
    steered,
    norm,
    chosen,
    small_box,
    base_box,
    small_qkv,
    query,
    pair,
    small_square,
    base_square,
    small_heads,
    base_heads,
    input_sems,
    attention_scratch,
    attention_sems,
    output_scratch,
    output_sems,
):
    group = lax.axis_index("grp")
    mine = lax.axis_index("tp")
    data = lax.axis_index("dp")
    place = group * size + mine
    count = 2 * size
    rows, small_width = small_box.shape[1:]
    base_width = base_box.shape[3]
    row_count, depth = small_cache.shape[2:4]
    parts = small_w.shape[1]
    half = jnp.bfloat16

    def greet():
        barrier = pltpu.get_barrier_semaphore()

        def call(step, carry):
            index = (place + step) % count
            pl.semaphore_signal(
                barrier,
                inc=1,
                device_id=(index // size, index % size, data),
                device_id_type=pl.DeviceIdType.MESH,
            )
            return carry

        lax.fori_loop(1, count, call, 0)
        pl.semaphore_wait(barrier, count - 1)

    cache = pltpu.VMEM((row_count, depth, CACHE), half)
    wide = pltpu.VMEM((row_count, LANES, CACHE), half)
    slice_width = pair_w.shape[1]

    def outer(small_keys, base_keys):
        fetch_keys, score, attend = attention_part(
            share,
            small_qkv,
            query,
            pair,
            lengths,
            small_cache,
            base_cache,
            small_heads,
            base_heads,
            small_keys,
            base_keys,
            *attention_scratch,
            attention_scratch[-1],
            *attention_sems,
        )

        def first(small_tiles, query_tiles, pair_tiles, small_total, query_total, pair_total, *tables):
            input_part(
                size,
                greet,
                fetch_keys,
                score,
                small_x,
                base_x,
                small_gain,
                base_gain,
                small_w,
                query_w,
                pair_w,
                lengths,
                small_qkv,
                query,
                pair,
                small_box,
                base_box,
                small_tiles,
                query_tiles,
                pair_tiles,
                small_total,
                query_total,
                pair_total,
                small_square,
                base_square,
                *tables,
                *input_sems,
            )

        table = pltpu.VMEM((rows, LANES), jnp.float32)
        pl.run_scoped(
            first,
            pltpu.VMEM((size, parts, small_width, depth), half),
            pltpu.VMEM((2, size, base_width, query_w.shape[1]), half),
            pltpu.VMEM((2, size, 2, slice_width, base_width), half),
            pltpu.VMEM((parts, rows, depth), jnp.float32),
            pltpu.VMEM((rows, query_w.shape[1]), jnp.float32),
            pltpu.VMEM((rows, 2 * LANES), jnp.float32),
            table,
            table,
            table,
            table,
        )
        def after(small_w_tiles, base_w_tiles):
            begin, start_small, rest = output_part(
                size,
                small_heads,
                base_heads,
                small_final,
                base_final,
                next_tokens,
                small_out_w,
                base_out_w,
                small_table,
                base_table,
                steered,
                norm,
                chosen,
                small_w_tiles,
                base_w_tiles,
                *output_scratch[:6],
                small_box,
                base_box,
                *output_scratch[6:9],
                small_square,
                base_square,
                *output_scratch[9:],
                *output_sems,
            )

            def between():
                start_small()

            def second(small_values, base_values):
                attend(begin, between, small_values, base_values)

            pl.run_scoped(second, cache, wide)
            vocab = base_table.shape[0]
            pl.run_scoped(
                rest,
                pltpu.VMEM((slots, 2, vocab, small_width), half),
                pltpu.VMEM((2, slots, vocab, base_width), half),
            )

        output_depth = base_out_w.shape[0]
        pl.run_scoped(
            after,
            pltpu.VMEM((size, depth, small_width), half),
            pltpu.VMEM((2, size, output_depth, base_width), half),
        )

    pl.run_scoped(outer, cache, wide)


def whole_stage(
    small_x,
    base_x,
    small_gain,
    base_gain,
    small_final,
    base_final,
    lengths,
    next_tokens,
    small_w,
    query_w,
    pair_w,
    small_cache,
    base_cache,
    small_out_w,
    base_out_w,
    small_table,
    base_table,
):
    size = lax.axis_size("tp")
    rows, small_width = small_x.shape
    base_width = base_x.shape[1]
    row_count, depth = small_cache.shape[2:4]
    base_depth = query_w.shape[1]
    slice_width = base_cache.shape[2]
    share = HD // slice_width
    copies = LANES // slice_width
    base_rows = 4 * (base_depth // slice_width)
    part_rows = max(8, 4 * (depth // HD))
    chunks = row_count // 8
    parts = small_w.shape[1]
    padded = rows // STEPS * (STEPS + 1)
    vocab = base_table.shape[0]
    stat_rows = rows + -rows % LANES
    slots = 3
    half = jnp.bfloat16
    wide = jnp.float32
    vmem = pl.BlockSpec(memory_space=pltpu.VMEM)
    smem = pl.BlockSpec(memory_space=pltpu.SMEM)
    hbm = pl.BlockSpec(memory_space=pl.ANY)
    dma = pltpu.SemaphoreType.DMA
    space = pltpu.VMEM
    return pl.pallas_call(
        functools.partial(whole_kernel, size, share, slots),
        in_specs=[hbm] * 2 + [vmem] * 4 + [smem] * 2 + [hbm] * 9,
        out_specs=[vmem] * 3,
        out_shape=[
            jax.ShapeDtypeStruct((rows, vocab), wide),
            jax.ShapeDtypeStruct((rows, LANES), wide),
            jax.ShapeDtypeStruct((row_count, LANES), wide),
        ],
        scratch_shapes=[
            space((size, rows, small_width), half),
            space((2, size, rows, base_width), half),
            space((parts, depth // LANES, padded, LANES), wide),
            space((base_depth // LANES, padded, LANES), wide),
            space((2, padded, LANES), wide),
            space((rows, LANES), wide),
            space((rows, LANES), wide),
            space((rows, depth), half),
            space((rows, base_depth), half),
            [dma((2,)), dma((size,)), dma((2, size)), dma((2, size))]
            + [dma((size,))] * 6,
            [
                space((row_count, part_rows, CACHE), wide),
                space((row_count, part_rows, 8), wide),
                space((row_count, part_rows, CACHE), half),
                space((row_count, part_rows, 8), wide),
                space((row_count, base_rows, CACHE), wide),
                space((row_count, base_rows, CACHE), half),
                space((share - 1, row_count, base_rows, CACHE), half),
                space((max(depth, base_depth) // LANES, padded, LANES), wide),
            ],
            [dma((2, chunks)), dma((2, copies)), dma((share - 1, chunks)), dma((share - 1, chunks))],
            [space((size, rows, small_width), half)] * 2
            + [space((size, rows, base_width), half)] * 4
            + [
                space((2, rows, vocab), wide),
                space((rows, vocab), wide),
                space((rows, vocab), wide),
                space((stat_rows, LANES), wide),
                space((2 * size, 8, stat_rows), wide),
                space((rows, LANES), jnp.int32),
            ],
            [
                dma((size,)),
                dma((2, size)),
                dma((size,)),
                dma((2, size)),
                dma((2, size)),
                dma((2, size)),
                dma((size,)),
                dma((size,)),
                dma((2, size)),
                dma((2, size)),
                dma((size,)),
                dma((size,)),
                dma((2,)),
                dma((2 * size,)),
                dma((2 * size,)),
            ],
        ],
        compiler_params=pltpu.CompilerParams(
            collective_id=0, has_side_effects=True, vmem_limit_bytes=VMEM_LIMIT
        ),
    )(
        small_x,
        base_x,
        small_gain.reshape(size, 1, small_width),
        base_gain.reshape(2 * size, 1, base_width),
        small_final.reshape(size, 1, small_width),
        base_final.reshape(2 * size, 1, base_width),
        lengths,
        next_tokens,
        small_w,
        query_w,
        pair_w,
        small_cache,
        base_cache,
        small_out_w,
        base_out_w,
        small_table,
        base_table,
    )


def finish_kernel(steered, norm, chosen, log_out, chosen_out):
    log_out[...] = steered[...] - norm[:, :1]

    @pl.when(pl.program_id(0) == 0)
    def _():
        chosen_out[...] = chosen[...].T[1:2]


def finish(steered, norm, chosen):
    rows, width = steered.shape
    tile = rows // STEPS
    tall = pl.BlockSpec((tile, width), lambda i: (i, 0))
    return pl.pallas_call(
        finish_kernel,
        grid=(STEPS,),
        in_specs=[
            tall,
            pl.BlockSpec((tile, LANES), lambda i: (i, 0)),
            pl.BlockSpec(chosen.shape, lambda i: (0, 0)),
        ],
        out_specs=[tall, pl.BlockSpec((1, chosen.shape[0]), lambda i: (0, 0))],
        out_shape=[
            jax.ShapeDtypeStruct(steered.shape, jnp.float32),
            jax.ShapeDtypeStruct((1, chosen.shape[0]), jnp.float32),
        ],
    )(steered, norm, chosen)


def body(
    base_inputs,
    small_inputs,
    base_norm_gain,
    base_query,
    base_keys_values,
    base_output,
    base_cache,
    base_final_gain,
    base_unembed,
    small_norm_gain,
    small_projections,
    small_output,
    small_cache,
    small_final_gain,
    small_unembed,
    lengths,
    next_tokens,
):
    row_count = lengths.shape[0]
    total_rows = STEPS * row_count
    vocab_width = base_unembed.shape[0]
    small_block = small_inputs.reshape(total_rows, -1)
    base_block = base_inputs.reshape(total_rows, -1)
    pair_weights = jnp.swapaxes(base_keys_values, 1, 2)
    steered, norm, chosen = whole_stage(
        small_block,
        base_block,
        small_norm_gain,
        base_norm_gain,
        small_final_gain,
        base_final_gain,
        lengths,
        next_tokens,
        small_projections,
        base_query,
        pair_weights,
        small_cache,
        base_cache,
        small_output,
        base_output,
        small_unembed,
        base_unembed,
    )
    log_probs, chosen = finish(steered, norm, chosen)
    return log_probs.reshape(STEPS, row_count, vocab_width), chosen.reshape(row_count)


def solution(mesh):
    placed = (
        P(None, "dp", ("grp", "tp")),
        P("grp", None, "dp", "tp"),
        P(),
        P(None, ("grp", "tp")),
        P(None, None, ("grp", "tp")),
        P(("grp", "tp"), None),
        P(None, "dp", ("grp", "tp"), None),
        P(),
        P(("grp", "tp"), None),
        P("grp", None),
        P("grp", None, None, "tp"),
        P("grp", "tp", None),
        P("grp", None, "dp", "tp", None),
        P("grp", None),
        P("grp", None, "tp", None),
        P("dp"),
        P(None, "dp"),
    )
    return jax.shard_map(
        body,
        mesh=mesh,
        in_specs=placed,
        out_specs=(P(None, "dp", ("grp", "tp")), P("dp")),
        check_vma=False,
    )
```
